128 devices in a mesh: clip: 16 (over y, x), cap: 8 (over z, core).
Axes of the slice: x: 4, y: 4, z: 4, core: 2. Of those that a mesh axis runs over, the one named last changes fastest.
Arguments:
- teacher_audio: bfloat16 [24576, 512], P(('clip', 'cap')), may hold values from -2 to 2
- teacher_text: bfloat16 [24576, 512], P(('cap', 'clip')), may hold values from -2 to 2
- student_audio: bfloat16 [24576, 512], P(('clip', 'cap')), may hold values from -2 to 2
- student_text: bfloat16 [24576, 512], P(('cap', 'clip')), may hold values from -2 to 2
Outputs:
- audio_grad: float32 [24576, 512], P(('clip', 'cap'))
- text_grad: float32 [24576, 512], P(('cap', 'clip'))
The draws below stay inside these ranges and needn't reach their ends.
All inputs are finite; a program needn't handle non-finite values.
Results may differ from the reference program's by a relative error of at most 0.0026.
Values may be sent and summed in bfloat16 or wider, within the bound.
No kernel may reach another device: no remote copies, remote signals or barrier semaphores. Data moves between devices by JAX's collectives and lax.ppermute only.
A program may use at most 128 MiB of HBM per device.

```python
import math
import jax
import jax.numpy as jnp
from jax import lax

D = 512
ITERS = 3
PAIRS = 24576


def embed_pair(key):
    key_audio = jax.random.fold_in(key, 0)
    key_text = jax.random.fold_in(key, 1)
    key_scale_a = jax.random.fold_in(key, 3)
    key_scale_t = jax.random.fold_in(key, 4)
    spread_base = 0.55 * D ** (-0.25)
    scale_range = 0.55
    audio_rows = spread_base * jnp.clip(jax.random.normal(key_audio, (PAIRS, D), jnp.float32), -4.0, 4.0)
    audio_rows = audio_rows * jnp.exp(jax.random.uniform(key_scale_a, (PAIRS, 1), jnp.float32, -scale_range, scale_range))
    text_rows = spread_base * jnp.clip(jax.random.normal(key_text, (PAIRS, D), jnp.float32), -4.0, 4.0)
    text_rows = text_rows * jnp.exp(jax.random.uniform(key_scale_t, (PAIRS, 1), jnp.float32, -scale_range, scale_range))
    return (audio_rows, text_rows)


def draw_teacher_audio(key, part):
    return embed_pair(jax.random.fold_in(key, 11))[0].astype(jnp.bfloat16)


def draw_teacher_text(key, part):
    return embed_pair(jax.random.fold_in(key, 11))[1].astype(jnp.bfloat16)


def draw_student_audio(key, part):
    return embed_pair(jax.random.fold_in(key, 23))[0].astype(jnp.bfloat16)


def draw_student_text(key, part):
    return embed_pair(jax.random.fold_in(key, 23))[1].astype(jnp.bfloat16)


def setup_inputs(seed: int = 0) -> dict:
    keys = jax.random.split(jax.random.key(seed), 5)
    return {
        "teacher_audio": draw_teacher_audio(jax.random.fold_in(keys[4], 71), 0),
        "teacher_text": draw_teacher_text(jax.random.fold_in(keys[4], 71), 0),
        "student_audio": draw_student_audio(jax.random.fold_in(keys[4], 71), 0),
        "student_text": draw_student_text(jax.random.fold_in(keys[4], 71), 0),
    }


def teacher_kernel(row_block, teacher_text):
    logits = 10.0 * jnp.dot(row_block, teacher_text.T, preferred_element_type=jnp.float32)
    return jnp.exp(logits - jnp.max(logits, axis=1, keepdims=True))


def reference(teacher_audio, teacher_text, student_audio, student_text):
    block_size = math.gcd(PAIRS, 1024)
    block_count = PAIRS // block_size
    audio_blocks = teacher_audio.reshape(block_count, block_size, D)
    student_blocks = student_audio.reshape(block_count, block_size, D)

    def first_pass(running, row_block):
        kernel = teacher_kernel(row_block, teacher_text)
        return running + jnp.sum(kernel, axis=0), None

    column, _ = lax.scan(first_pass, jnp.zeros((PAIRS,), jnp.float32), audio_blocks)
    column_scale = 1.0 / column
    weights_row = None
    for sweep_index in range(ITERS):
        column_scale = 1.0 / column

        def sweep(running, row_block, scale_now=column_scale):
            kernel = teacher_kernel(row_block, teacher_text)
            weights = 1.0 / jnp.dot(kernel, scale_now, precision=lax.Precision.HIGHEST)
            return running + jnp.dot(weights, kernel, precision=lax.Precision.HIGHEST), weights

        column, weights_row = lax.scan(sweep, jnp.zeros((PAIRS,), jnp.float32), audio_blocks)

    def final_pass(running, inputs):
        row_block, weight_block, student_block = inputs
        kernel = teacher_kernel(row_block, teacher_text)
        target = (weight_block[:, None] * kernel) * column_scale[None, :]
        logits = 10.0 * jnp.dot(student_block, student_text.T, preferred_element_type=jnp.float32)
        student_exp = jnp.exp(logits - jnp.max(logits, axis=1, keepdims=True))
        student_prob = student_exp / jnp.sum(student_exp, axis=1, keepdims=True)
        residual = (student_prob - target).astype(jnp.bfloat16)
        audio_part = 10.0 * jnp.dot(residual, student_text, preferred_element_type=jnp.float32)
        text_part = 10.0 * jnp.dot(residual.T, student_block, preferred_element_type=jnp.float32)
        return running + text_part, audio_part

    text_grad, audio_parts = lax.scan(final_pass, jnp.zeros((PAIRS, D), jnp.float32),
                                      (audio_blocks, weights_row, student_blocks))
    return audio_parts.reshape(PAIRS, D), text_grad
```

```python
import functools

import jax
import jax.numpy as jnp
from jax import lax
from jax.experimental import pallas as pl
from jax.experimental.pallas import tpu as pltpu
from jax.sharding import PartitionSpec as P

ITERS = 3
LANES = 128
VMEM = pl.BlockSpec(memory_space=pltpu.VMEM)
LIMIT = 8 * 1024 * 1024


def params(limit=LIMIT):
    return pltpu.CompilerParams(vmem_limit_bytes=limit)


def lanes_of(ref, block):
    return ref[pl.ds(block * LANES, LANES), :].T


def spread_rows(vec, ref):
    for block in range(vec.shape[0]):
        row = jnp.broadcast_to(vec[block : block + 1, :], (LANES, LANES))
        ref[pl.ds(block * LANES, LANES), :] = row.T


def spread_cols(vec):
    return jnp.concatenate(
        [jnp.broadcast_to(vec[g : g + 1, :], (8, LANES)) for g in range(vec.shape[0])], axis=1
    )


def repeat_lanes(col, groups):
    return jnp.concatenate([col] * groups, axis=1)


def fold_lanes(x, op):
    parts = [x[:, g * LANES : (g + 1) * LANES] for g in range(x.shape[1] // LANES)]
    while len(parts) > 1:
        parts = [op(*parts[k : k + 2]) if k + 1 < len(parts) else parts[k] for k in range(0, len(parts), 2)]
    return parts[0]


def logits_kernel(audio_ref, text_ref, logits_ref, max_ref, part_ref):
    rows, columns = logits_ref.shape
    step, width = 256, 512

    def block(i, _):
        base = pl.multiple_of(i * step, step)
        left = audio_ref[pl.ds(base, step), :]
        best = None
        for j in range(columns // width):
            x = 10.0 * lax.dot_general(
                left,
                text_ref[pl.ds(j * width, width), :],
                (((1,), (1,)), ((), ())),
                preferred_element_type=jnp.float32,
            )
            logits_ref[pl.ds(base, step), pl.ds(j * width, width)] = x
            folded = fold_lanes(x, jnp.maximum)
            best = folded if best is None else jnp.maximum(best, folded)
        part_ref[pl.ds(base, step), :] = best
        return 0

    lax.fori_loop(0, rows // step, block, 0)
    for b in range(rows // LANES):
        top = jnp.max(lanes_of(part_ref, b), axis=0, keepdims=True)
        for k in range(max_ref.shape[0]):
            max_ref[k, b : b + 1, :] = top


def teacher_logits(audio, text, peers):
    rows, columns = audio.shape[0], text.shape[0]
    return pl.pallas_call(
        logits_kernel,
        out_shape=(
            pltpu.VMEM((rows, columns), jnp.float32),
            jax.ShapeDtypeStruct((peers, rows // LANES, LANES), jnp.float32),
        ),
        in_specs=[VMEM, VMEM],
        out_specs=(VMEM, VMEM),
        scratch_shapes=[pltpu.VMEM((rows, LANES), jnp.float32)],
        compiler_params=params(),
        name="logits",
    )(audio, text)


def put_columns(acc, sum_ref, out_ref):
    groups = sum_ref.shape[0]
    for g in range(groups):
        sum_ref[g : g + 1, :] = jnp.sum(acc[:, g * LANES : (g + 1) * LANES], axis=0, keepdims=True)
    total = sum_ref[...]
    for k in range(out_ref.shape[0]):
        out_ref[k] = total


def exp_kernel(max_ref, logits_ref, kernel_ref, out_ref, col_ref, sum_ref):
    rows, columns = logits_ref.shape
    spread_rows(jnp.max(max_ref[...], axis=0), col_ref)

    def step(i, acc):
        at = pl.ds(pl.multiple_of(i * 8, 8), 8)
        k = jnp.exp(logits_ref[at, :] - repeat_lanes(col_ref[at, :], columns // LANES))
        kernel_ref[at, :] = k
        return acc + k

    acc = lax.fori_loop(0, rows // 8, step, jnp.zeros((8, columns), jnp.float32), unroll=4)
    put_columns(acc, sum_ref, out_ref)


def exp_columns(maxima, logits, peers):
    rows, columns = logits.shape
    return pl.pallas_call(
        exp_kernel,
        out_shape=(
            pltpu.VMEM((rows, columns), jnp.float32),
            jax.ShapeDtypeStruct((peers, columns // LANES, LANES), jnp.float32),
        ),
        in_specs=[VMEM, VMEM],
        out_specs=(VMEM, VMEM),
        scratch_shapes=[
            pltpu.VMEM((rows, LANES), jnp.float32),
            pltpu.VMEM((columns // LANES, LANES), jnp.float32),
        ],
        input_output_aliases={1: 0},
        compiler_params=params(),
        name="exp_columns",
    )(maxima, resident(logits))


def row_kernel(*refs):
    parts_ref, kernel_ref = refs[:2]
    stat_ref = refs[2] if len(refs) == 6 else None
    out_ref, scale_ref, part_ref = refs[-3:]
    rows, columns = kernel_ref.shape
    blocks = rows // LANES
    scale_ref[...] = 1.0 / jnp.sum(parts_ref[...], axis=0)
    scale = spread_cols(scale_ref[...])

    def step(i, _):
        at = pl.ds(pl.multiple_of(i * 8, 8), 8)
        part_ref[at, :] = fold_lanes(kernel_ref[at, :] * scale, jnp.add)
        return 0

    lax.fori_loop(0, rows // 8, step, 0, unroll=4)
    for b in range(blocks):
        total = jnp.sum(lanes_of(part_ref, b), axis=0, keepdims=True)
        for k in range(out_ref.shape[0]):
            out_ref[k, b : b + 1, :] = total
    if stat_ref is not None:
        for k in range(out_ref.shape[0]):
            out_ref[k, blocks:, :] = stat_ref[...]


def row_sums(parts, kernel, peers, stats=None):
    rows, columns = kernel.shape
    extra = () if stats is None else (stats,)
    return pl.pallas_call(
        row_kernel,
        out_shape=(
            jax.ShapeDtypeStruct((peers, rows // LANES * (3 if extra else 1), LANES), jnp.float32),
            jax.ShapeDtypeStruct((columns // LANES, LANES), jnp.float32),
        ),
        in_specs=[VMEM, VMEM] + [VMEM] * len(extra),
        out_specs=(VMEM, VMEM),
        scratch_shapes=[pltpu.VMEM((rows, LANES), jnp.float32)],
        compiler_params=params(),
        name="row_sums",
    )(parts, resident(kernel), *extra)


def column_kernel(parts_ref, kernel_ref, out_ref, col_ref, sum_ref):
    rows, columns = kernel_ref.shape
    spread_rows(1.0 / jnp.sum(parts_ref[...], axis=0), col_ref)

    def step(i, acc):
        at = pl.ds(pl.multiple_of(i * 8, 8), 8)
        return acc + kernel_ref[at, :] * repeat_lanes(col_ref[at, :], columns // LANES)

    acc = lax.fori_loop(0, rows // 8, step, jnp.zeros((8, columns), jnp.float32), unroll=4)
    put_columns(acc, sum_ref, out_ref)


def column_sums(parts, kernel, peers):
    rows, columns = kernel.shape
    return pl.pallas_call(
        column_kernel,
        out_shape=jax.ShapeDtypeStruct((peers, columns // LANES, LANES), jnp.float32),
        in_specs=[VMEM, VMEM],
        out_specs=VMEM,
        scratch_shapes=[
            pltpu.VMEM((rows, LANES), jnp.float32),
            pltpu.VMEM((columns // LANES, LANES), jnp.float32),
        ],
        compiler_params=params(),
        name="column_sums",
    )(parts, resident(kernel))


def student_kernel(audio_ref, text_ref, exp_ref, stat_ref, part_ref):
    step, columns = exp_ref.shape
    width = 512
    here = step // LANES
    blocks = stat_ref.shape[0] // 2
    i = pl.program_id(0)
    best = None
    for j in range(columns // width):
        x = 10.0 * lax.dot_general(
            audio_ref[...],
            text_ref[pl.ds(j * width, width), :],
            (((1,), (1,)), ((), ())),
            preferred_element_type=jnp.float32,
        )
        exp_ref[:, pl.ds(j * width, width)] = x
        folded = fold_lanes(x, jnp.maximum)
        best = folded if best is None else jnp.maximum(best, folded)
    part_ref[...] = best
    for b in range(here):
        top = jnp.max(lanes_of(part_ref, b), axis=0, keepdims=True)
        stat_ref[pl.ds(i * here + b, 1), :] = top
        part_ref[pl.ds(b * LANES, LANES), :] = jnp.broadcast_to(top, (LANES, LANES)).T

    def exps(r, _):
        at = pl.ds(pl.multiple_of(r * 8, 8), 8)
        e = jnp.exp(exp_ref[at, :] - repeat_lanes(part_ref[at, :], columns // LANES))
        exp_ref[at, :] = e
        part_ref[at, :] = fold_lanes(e, jnp.add)
        return 0

    lax.fori_loop(0, step // 8, exps, 0, unroll=4)
    for b in range(here):
        total = jnp.sum(lanes_of(part_ref, b), axis=0, keepdims=True)
        stat_ref[pl.ds(blocks + i * here + b, 1), :] = total


def student_softmax(audio, text):
    rows, columns, depth = audio.shape[0], text.shape[0], audio.shape[1]
    step = 256
    return pl.pallas_call(
        student_kernel,
        grid=(rows // step,),
        out_shape=(
            jax.ShapeDtypeStruct((rows, columns), jnp.float32),
            jax.ShapeDtypeStruct((2 * (rows // LANES), LANES), jnp.float32),
        ),
        in_specs=[
            pl.BlockSpec((step, depth), lambda i: (i, 0)),
            pl.BlockSpec((columns, depth), lambda i: (0, 0), pipeline_mode=pl.Buffered(1)),
        ],
        out_specs=(
            pl.BlockSpec((step, columns), lambda i: (i, 0)),
            pl.BlockSpec((2 * (rows // LANES), LANES), lambda i: (0, 0)),
        ),
        scratch_shapes=[pltpu.VMEM((step, LANES), jnp.float32)],
        compiler_params=params(16 * 1024 * 1024),
        cost_estimate=pl.CostEstimate(
            flops=2 * rows * columns * depth, bytes_accessed=4 * rows * columns, transcendentals=rows * columns
        ),
        name="student_softmax",
    )(audio, text)


def residual_kernel(
    rows_ref, scale_ref, own_ref, kernel_ref, exp_ref, audio_ref, text_ref,
    audio_out_ref, text_out_ref, weight_ref, prob_ref, residual_ref, acc_ref,
):
    step, columns = exp_ref.shape
    blocks = own_ref.shape[0] // 2
    i = pl.program_id(0)

    @pl.when(i == 0)
    def _():
        spread_rows(1.0 / jnp.sum(rows_ref[:, :blocks, :], axis=0), weight_ref)
        tops = rows_ref[:, blocks : 2 * blocks, :]
        top = jnp.max(tops, axis=0)
        total = jnp.sum(jnp.exp(tops - top[None]) * rows_ref[:, 2 * blocks :, :], axis=0)
        spread_rows(jnp.exp(own_ref[:blocks, :] - top) / total, prob_ref)

        def clear(k, _):
            acc_ref[pl.ds(pl.multiple_of(k * 64, 64), 64), :] = jnp.zeros((64, acc_ref.shape[1]), jnp.float32)
            return 0

        lax.fori_loop(0, columns // 64, clear, 0)

    scale = spread_cols(scale_ref[...])

    def part(j, _):
        out = []
        for half in range(2):
            off = pl.multiple_of(j * 16 + half * 8, 8)
            at = pl.ds(off, 8)
            whole = pl.ds(pl.multiple_of(i * step + off, 8), 8)
            weight = repeat_lanes(weight_ref[whole, :], columns // LANES)
            prob = repeat_lanes(prob_ref[whole, :], columns // LANES)
            out.append(exp_ref[at, :] * prob - (weight * kernel_ref[whole, :]) * scale)
        residual_ref[pl.ds(pl.multiple_of(j * 16, 16), 16), :] = jnp.concatenate(out, axis=0).astype(jnp.bfloat16)
        return 0

    lax.fori_loop(0, step // 16, part, 0)
    for j in range(columns // 512):
        acc_ref[pl.ds(j * 512, 512), :] += lax.dot_general(
            residual_ref[:, pl.ds(j * 512, 512)],
            audio_ref[...],
            (((0,), (0,)), ((), ())),
            preferred_element_type=jnp.float32,
        )
    audio_out_ref[...] = 10.0 * jnp.dot(residual_ref[...], text_ref[...], preferred_element_type=jnp.float32)

    @pl.when(i == pl.num_programs(0) - 1)
    def _():
        def finish(k, _):
            at = pl.ds(pl.multiple_of(k * 64, 64), 64)
            text_out_ref[at, :] = (10.0 * acc_ref[at, :]).astype(text_out_ref.dtype)
            return 0

        lax.fori_loop(0, columns // 64, finish, 0)


def residual_grads(row_parts, scale, own, kernel, exps, audio, text, dtype):
    rows, columns = kernel.shape
    depth = audio.shape[1]
    step = 256
    return pl.pallas_call(
        residual_kernel,
        grid=(rows // step,),
        out_shape=(
            jax.ShapeDtypeStruct((rows, depth), jnp.float32),
            jax.ShapeDtypeStruct((columns, depth), dtype),
        ),
        in_specs=[VMEM] * 4
        + [
            pl.BlockSpec((step, columns), lambda i: (i, 0)),
            pl.BlockSpec((step, depth), lambda i: (i, 0)),
            pl.BlockSpec((columns, depth), lambda i: (0, 0), pipeline_mode=pl.Buffered(1)),
        ],
        out_specs=(
            pl.BlockSpec((step, depth), lambda i: (i, 0)),
            pl.BlockSpec((columns, depth), lambda i: (0, 0)),
        ),
        scratch_shapes=[
            pltpu.VMEM((rows, LANES), jnp.float32),
            pltpu.VMEM((rows, LANES), jnp.float32),
            pltpu.VMEM((step, columns), jnp.bfloat16),
            pltpu.VMEM((columns, depth), jnp.float32),
        ],
        compiler_params=params(36 * 1024 * 1024),
        name="residual_grads",
    )(row_parts, scale, own, resident(kernel), exps, audio, text)


def resident(x):
    return pltpu.with_memory_space_constraint(x, pltpu.VMEM)


def gather_a2a(x, axis, n):
    spread = jnp.broadcast_to(x[None], (n, *x.shape))
    return lax.all_to_all(spread, axis, 0, 0).reshape(n * x.shape[0], x.shape[1])


def swap(x, axis):
    return lax.all_to_all(x, axis, 0, 0)


def body(clips, caps, teacher_audio, teacher_text, student_audio, student_text):
    audio_t = lax.all_gather(teacher_audio, "cap", axis=0, tiled=True)
    text_t = gather_a2a(teacher_text, "clip", clips)
    text_s = lax.all_gather(student_text, "clip", axis=0, tiled=True)
    audio_s = lax.all_gather(student_audio, "cap", axis=0, tiled=True)
    logits, maxima = teacher_logits(audio_t, text_t, caps)
    kernel, columns = exp_columns(swap(maxima, "cap"), logits, clips)
    stats = None
    for sweep_index in range(ITERS):
        last = sweep_index + 1 == ITERS
        if last:
            exps, stats = student_softmax(audio_s, text_s)
        row_parts, scale = row_sums(swap(columns, "clip"), kernel, caps, stats)
        row_parts = swap(row_parts, "cap")
        if not last:
            columns = column_sums(row_parts, kernel, clips)
    audio_part, text_part = residual_grads(row_parts, scale, stats, kernel, exps, audio_s, text_s, jnp.bfloat16)
    audio_grad = lax.psum_scatter(audio_part, "cap", scatter_dimension=0, tiled=True)
    text_parts = swap(text_part.reshape(clips, -1, text_part.shape[1]), "clip")
    text_grad = jnp.sum(text_parts.astype(jnp.float32), axis=0)
    return audio_grad, text_grad


def solution(mesh):
    placed = (
        P(("clip", "cap"), None),
        P(("cap", "clip"), None),
        P(("clip", "cap"), None),
        P(("cap", "clip"), None),
    )
    return jax.shard_map(
        functools.partial(body, mesh.shape["clip"], mesh.shape["cap"]),
        mesh=mesh,
        in_specs=placed,
        out_specs=(P(("clip", "cap"), None), P(("cap", "clip"), None)),
        check_vma=False,
    )
```

```python
import functools

import jax
import jax.numpy as jnp
from jax import lax
from jax.experimental import pallas as pl
from jax.experimental.pallas import tpu as pltpu
from jax.sharding import PartitionSpec as P

ITERS = 3
LANES = 128
WIDTH = 512
VMEM = pl.BlockSpec(memory_space=pltpu.VMEM)
LIMIT = 8 * 1024 * 1024


def params(limit=LIMIT):
    return pltpu.CompilerParams(vmem_limit_bytes=limit)


def lanes_of(ref, block):
    return ref[pl.ds(block * LANES, LANES), :].T


def spread_rows(vec, ref):
    for block in range(vec.shape[0]):
        row = jnp.broadcast_to(vec[block : block + 1, :], (LANES, LANES))
        ref[pl.ds(block * LANES, LANES), :] = row.T


def spread_cols(vec):
    return jnp.concatenate(
        [jnp.broadcast_to(vec[g : g + 1, :], (8, LANES)) for g in range(vec.shape[0])], axis=1
    )


def repeat_lanes(col, groups):
    return jnp.concatenate([col] * groups, axis=1)


def fold_lanes(x, op):
    parts = [x[:, g * LANES : (g + 1) * LANES] for g in range(x.shape[1] // LANES)]
    while len(parts) > 1:
        parts = [op(*parts[k : k + 2]) if k + 1 < len(parts) else parts[k] for k in range(0, len(parts), 2)]
    return parts[0]


def contract_last(left, right):
    return lax.dot_general(left, right, (((1,), (1,)), ((), ())), preferred_element_type=jnp.float32)


def logits_kernel(audio_ref, text_ref, logits_ref, max_ref, part_ref):
    rows, columns = logits_ref.shape
    step = 256

    def block(i, _):
        base = pl.multiple_of(i * step, step)
        left = audio_ref[pl.ds(base, step), :]
        best = None
        for j in range(columns // WIDTH):
            at = j * WIDTH
            x = 10.0 * contract_last(left, text_ref[pl.ds(at, WIDTH), :])
            logits_ref[pl.ds(base, step), pl.ds(at, WIDTH)] = x
            folded = fold_lanes(x, jnp.maximum)
            best = folded if best is None else jnp.maximum(best, folded)
        part_ref[pl.ds(base, step), :] = best
        return 0

    lax.fori_loop(0, rows // step, block, 0)
    for b in range(rows // LANES):
        top = jnp.max(lanes_of(part_ref, b), axis=0, keepdims=True)
        for k in range(max_ref.shape[0]):
            max_ref[k, b : b + 1, :] = top


def teacher_logits(audio, text, peers):
    rows, columns = audio.shape[0], text.shape[0]
    return pl.pallas_call(
        logits_kernel,
        out_shape=(
            pltpu.VMEM((rows, columns), jnp.float32),
            jax.ShapeDtypeStruct((peers, rows // LANES, LANES), jnp.float32),
        ),
        in_specs=[VMEM, VMEM],
        out_specs=(VMEM, VMEM),
        scratch_shapes=[pltpu.VMEM((rows, LANES), jnp.float32)],
        compiler_params=params(),
        name="logits",
    )(audio, text)


def put_columns(acc, sum_ref, out_ref):
    groups = sum_ref.shape[0]
    for g in range(groups):
        sum_ref[g : g + 1, :] = jnp.sum(acc[:, g * LANES : (g + 1) * LANES], axis=0, keepdims=True)
    total = sum_ref[...]
    for k in range(out_ref.shape[0]):
        out_ref[k] = total


def exp_kernel(max_ref, logits_ref, kernel_ref, out_ref, col_ref, sum_ref):
    rows, columns = logits_ref.shape
    spread_rows(jnp.max(max_ref[...], axis=0), col_ref)

    def step(i, acc):
        at = pl.ds(pl.multiple_of(i * 8, 8), 8)
        k = jnp.exp(logits_ref[at, :] - repeat_lanes(col_ref[at, :], columns // LANES))
        kernel_ref[at, :] = k
        return acc + k

    acc = lax.fori_loop(0, rows // 8, step, jnp.zeros((8, columns), jnp.float32), unroll=4)
    put_columns(acc, sum_ref, out_ref)


def exp_columns(maxima, logits, peers):
    rows, columns = logits.shape
    return pl.pallas_call(
        exp_kernel,
        out_shape=(
            pltpu.VMEM((rows, columns), jnp.float32),
            jax.ShapeDtypeStruct((peers, columns // LANES, LANES), jnp.float32),
        ),
        in_specs=[VMEM, VMEM],
        out_specs=(VMEM, VMEM),
        scratch_shapes=[
            pltpu.VMEM((rows, LANES), jnp.float32),
            pltpu.VMEM((columns // LANES, LANES), jnp.float32),
        ],
        input_output_aliases={1: 0},
        compiler_params=params(),
        name="exp_columns",
    )(maxima, resident(logits))


def row_kernel(parts_ref, kernel_ref, out_ref, part_ref):
    rows = kernel_ref.shape[0]
    scale = spread_cols(1.0 / jnp.sum(parts_ref[...], axis=0))

    def step(i, _):
        at = pl.ds(pl.multiple_of(i * 8, 8), 8)
        part_ref[at, :] = fold_lanes(kernel_ref[at, :] * scale, jnp.add)
        return 0

    lax.fori_loop(0, rows // 8, step, 0, unroll=4)
    for b in range(rows // LANES):
        total = jnp.sum(lanes_of(part_ref, b), axis=0, keepdims=True)
        for k in range(out_ref.shape[0]):
            out_ref[k, b : b + 1, :] = total


def row_sums(parts, kernel, peers):
    rows = kernel.shape[0]
    return pl.pallas_call(
        row_kernel,
        out_shape=jax.ShapeDtypeStruct((peers, rows // LANES, LANES), jnp.float32),
        in_specs=[VMEM, VMEM],
        out_specs=VMEM,
        scratch_shapes=[pltpu.VMEM((rows, LANES), jnp.float32)],
        compiler_params=params(),
        name="row_sums",
    )(parts, resident(kernel))


def last_row_kernel(parts_ref, kernel_ref, stat_ref, out_ref, scale_ref, keep_ref, part_ref):
    step, columns = kernel_ref.shape
    here = step // LANES
    blocks = stat_ref.shape[0] // 2
    i = pl.program_id(0)

    @pl.when(i == 0)
    def _():
        scale_ref[...] = 1.0 / jnp.sum(parts_ref[...], axis=0)
        for k in range(out_ref.shape[0]):
            out_ref[k, blocks:, :] = stat_ref[...]

    scale = spread_cols(scale_ref[...])

    def rows(r, _):
        at = pl.ds(pl.multiple_of(r * 8, 8), 8)
        k = kernel_ref[at, :]
        keep_ref[pl.ds(pl.multiple_of(i * step + r * 8, 8), 8), :] = k
        part_ref[at, :] = fold_lanes(k * scale, jnp.add)
        return 0

    lax.fori_loop(0, step // 8, rows, 0, unroll=4)
    for b in range(here):
        total = jnp.sum(lanes_of(part_ref, b), axis=0, keepdims=True)
        for k in range(out_ref.shape[0]):
            out_ref[k, pl.ds(i * here + b, 1), :] = total


def last_row_sums(parts, kernel, stats, peers):
    rows, columns = kernel.shape
    step = 256
    return pl.pallas_call(
        last_row_kernel,
        grid=(rows // step,),
        out_shape=(
            jax.ShapeDtypeStruct((peers, 3 * (rows // LANES), LANES), jnp.float32),
            jax.ShapeDtypeStruct((columns // LANES, LANES), jnp.float32),
            pltpu.VMEM((rows, columns), jnp.float32),
        ),
        in_specs=[VMEM, pl.BlockSpec((step, columns), lambda i: (i, 0)), VMEM],
        out_specs=(
            pl.BlockSpec((peers, 3 * (rows // LANES), LANES), lambda i: (0, 0, 0)),
            pl.BlockSpec((columns // LANES, LANES), lambda i: (0, 0)),
            VMEM,
        ),
        scratch_shapes=[pltpu.VMEM((step, LANES), jnp.float32)],
        compiler_params=params(12 * 1024 * 1024),
        name="last_row_sums",
    )(parts, streamed(kernel), stats)


def column_kernel(parts_ref, kernel_ref, out_ref, col_ref, sum_ref):
    rows, columns = kernel_ref.shape
    spread_rows(1.0 / jnp.sum(parts_ref[...], axis=0), col_ref)

    def step(i, acc):
        at = pl.ds(pl.multiple_of(i * 8, 8), 8)
        return acc + kernel_ref[at, :] * repeat_lanes(col_ref[at, :], columns // LANES)

    acc = lax.fori_loop(0, rows // 8, step, jnp.zeros((8, columns), jnp.float32), unroll=4)
    put_columns(acc, sum_ref, out_ref)


def column_sums(parts, kernel, peers):
    rows, columns = kernel.shape
    return pl.pallas_call(
        column_kernel,
        out_shape=jax.ShapeDtypeStruct((peers, columns // LANES, LANES), jnp.float32),
        in_specs=[VMEM, VMEM],
        out_specs=VMEM,
        scratch_shapes=[
            pltpu.VMEM((rows, LANES), jnp.float32),
            pltpu.VMEM((columns // LANES, LANES), jnp.float32),
        ],
        compiler_params=params(),
        name="column_sums",
    )(parts, resident(kernel))


def student_kernel(audio_ref, text_ref, exp_ref, stat_ref, logits_ref):
    step, columns = exp_ref.shape
    here = step // LANES
    blocks = stat_ref.shape[0] // 2
    i = pl.program_id(0)
    best = None
    for j in range(columns // WIDTH):
        x = 10.0 * contract_last(audio_ref[...], text_ref[pl.ds(j * WIDTH, WIDTH), :])
        logits_ref[:, pl.ds(j * WIDTH, WIDTH)] = x
        folded = fold_lanes(x, jnp.maximum)
        best = folded if best is None else jnp.maximum(best, folded)
    for b in range(here):
        rows = pl.ds(b * LANES, LANES)
        top = jnp.max(best[b * LANES : (b + 1) * LANES, :].T, axis=0, keepdims=True)
        stat_ref[pl.ds(i * here + b, 1), :] = top
        top = repeat_lanes(jnp.broadcast_to(top, (LANES, LANES)).T, WIDTH // LANES)
        total = None
        for j in range(columns // WIDTH):
            e = jnp.exp(logits_ref[rows, pl.ds(j * WIDTH, WIDTH)] - top)
            exp_ref[rows, pl.ds(j * WIDTH, WIDTH)] = e
            folded = fold_lanes(e, jnp.add)
            total = folded if total is None else total + folded
        stat_ref[pl.ds(blocks + i * here + b, 1), :] = jnp.sum(total.T, axis=0, keepdims=True)


def student_softmax(audio, text):
    rows, columns, depth = audio.shape[0], text.shape[0], audio.shape[1]
    step = 256
    return pl.pallas_call(
        student_kernel,
        grid=(rows // step,),
        out_shape=(
            pltpu.HBM((rows, columns), jnp.float32),
            jax.ShapeDtypeStruct((2 * (rows // LANES), LANES), jnp.float32),
        ),
        in_specs=[
            pl.BlockSpec((step, depth), lambda i: (i, 0)),
            pl.BlockSpec((columns, depth), lambda i: (0, 0), pipeline_mode=pl.Buffered(1)),
        ],
        out_specs=(
            pl.BlockSpec((step, columns), lambda i: (i, 0)),
            pl.BlockSpec((2 * (rows // LANES), LANES), lambda i: (0, 0)),
        ),
        scratch_shapes=[pltpu.VMEM((step, columns), jnp.float32)],
        compiler_params=params(20 * 1024 * 1024),
        cost_estimate=pl.CostEstimate(
            flops=2 * rows * columns * depth, bytes_accessed=4 * rows * columns, transcendentals=rows * columns
        ),
        name="student_softmax",
    )(streamed(audio), streamed(text))


def residual_kernel(
    rows_ref, scale_ref, own_ref, kernel_ref, exp_ref, audio_ref, text_ref,
    audio_out_ref, text_out_ref, weight_ref, prob_ref, residual_ref,
):
    rows, width = exp_ref.shape
    blocks = own_ref.shape[0] // 2
    step = 256
    i = pl.program_id(0)

    @pl.when(i == 0)
    def _():
        spread_rows(1.0 / jnp.sum(rows_ref[:, :blocks, :], axis=0), weight_ref)
        tops = rows_ref[:, blocks : 2 * blocks, :]
        top = jnp.max(tops, axis=0)
        total = jnp.sum(jnp.exp(tops - top[None]) * rows_ref[:, 2 * blocks :, :], axis=0)
        spread_rows(jnp.exp(own_ref[:blocks, :] - top) / total, prob_ref)
        audio_out_ref[...] = jnp.zeros_like(audio_out_ref)

    groups = width // LANES
    columns = pl.ds(pl.multiple_of(i * width, width), width)
    scale = jnp.concatenate(
        [jnp.broadcast_to(scale_ref[pl.ds(i * groups + g, 1), :], (8, LANES)) for g in range(groups)], axis=1
    )
    scale = jnp.concatenate([scale] * (step // 8), axis=0)

    def block(k, _):
        at = pl.ds(pl.multiple_of(k * step, step), step)
        target = (repeat_lanes(weight_ref[at, :], groups) * kernel_ref[at, columns]) * scale
        residual = (exp_ref[at, :] * repeat_lanes(prob_ref[at, :], groups) - target).astype(jnp.bfloat16)
        residual_ref[at, :] = residual
        audio_out_ref[at, :] += jnp.dot(residual, text_ref[...], preferred_element_type=jnp.float32)
        return 0

    lax.fori_loop(0, rows // step, block, 0)
    grad = lax.dot_general(
        residual_ref[...], audio_ref[...], (((0,), (0,)), ((), ())), preferred_element_type=jnp.float32
    )
    text_out_ref[columns, :] = (10.0 * grad).astype(text_out_ref.dtype)

    @pl.when(i == pl.num_programs(0) - 1)
    def _():
        audio_out_ref[...] = 10.0 * audio_out_ref[...]


def residual_grads(row_parts, scale, own, kernel, exps, audio, text, dtype):
    rows, columns = kernel.shape
    depth = audio.shape[1]
    width = 2 * WIDTH
    return pl.pallas_call(
        residual_kernel,
        grid=(columns // width,),
        out_shape=(
            jax.ShapeDtypeStruct((rows, depth), jnp.float32),
            pltpu.VMEM((columns, depth), dtype),
        ),
        in_specs=[VMEM] * 4
        + [
            pl.BlockSpec((rows, width), lambda i: (0, i)),
            pl.BlockSpec((rows, depth), lambda i: (0, 0), pipeline_mode=pl.Buffered(1)),
            pl.BlockSpec((width, depth), lambda i: (i, 0)),
        ],
        out_specs=(pl.BlockSpec((rows, depth), lambda i: (0, 0)), VMEM),
        scratch_shapes=[
            pltpu.VMEM((rows, LANES), jnp.float32),
            pltpu.VMEM((rows, LANES), jnp.float32),
            pltpu.VMEM((rows, width), jnp.bfloat16),
        ],
        compiler_params=params(36 * 1024 * 1024),
        name="residual_grads",
    )(row_parts, scale, own, resident(kernel), streamed(exps), audio, text)


def streamed(x):
    return pltpu.with_memory_space_constraint(x, pltpu.HBM)


def resident(x):
    return pltpu.with_memory_space_constraint(x, pltpu.VMEM)


def gather_a2a(x, axis, n):
    spread = jnp.broadcast_to(x[None], (n, *x.shape))
    return lax.all_to_all(spread, axis, 0, 0).reshape(n * x.shape[0], x.shape[1])


def swap(x, axis):
    return lax.all_to_all(x, axis, 0, 0)


def body(clips, caps, teacher_audio, teacher_text, student_audio, student_text):
    text_t = lax.all_gather(teacher_text, "clip", axis=0, tiled=True)
    audio_t = gather_a2a(teacher_audio, "cap", caps)
    student_audio, student_text, audio_t = lax.optimization_barrier((student_audio, student_text, audio_t))
    audio_s = gather_a2a(student_audio, "cap", caps)
    audio_s, text_t = lax.optimization_barrier((audio_s, text_t))
    text_s = lax.all_gather(student_text, "clip", axis=0, tiled=True)
    logits, maxima = teacher_logits(audio_t, text_t, caps)
    kernel, columns = exp_columns(swap(maxima, "cap"), logits, clips)
    for _ in range(ITERS - 1):
        row_parts = row_sums(swap(columns, "clip"), kernel, caps)
        columns = column_sums(swap(row_parts, "cap"), kernel, clips)
    exps, stats = student_softmax(audio_s, text_s)
    row_parts, scale, kernel = last_row_sums(swap(columns, "clip"), kernel, stats, caps)
    row_parts = swap(row_parts, "cap")
    audio_part, text_part = residual_grads(
        row_parts, scale, stats, kernel, exps, audio_s, text_s, jnp.bfloat16
    )
    audio_grad = lax.psum_scatter(audio_part, "cap", scatter_dimension=0, tiled=True)
    text_parts = swap(text_part.reshape(clips, -1, text_part.shape[1]), "clip")
    text_grad = jnp.sum(text_parts.astype(jnp.float32), axis=0)
    return audio_grad, text_grad


def solution(mesh):
    placed = (
        P(("clip", "cap"), None),
        P(("cap", "clip"), None),
        P(("clip", "cap"), None),
        P(("cap", "clip"), None),
    )
    return jax.shard_map(
        functools.partial(body, mesh.shape["clip"], mesh.shape["cap"]),
        mesh=mesh,
        in_specs=placed,
        out_specs=(P(("clip", "cap"), None), P(("cap", "clip"), None)),
        check_vma=False,
    )
```

```python
import functools

import jax
import jax.numpy as jnp
from jax import lax
from jax.experimental import pallas as pl
from jax.experimental.pallas import tpu as pltpu
from jax.sharding import PartitionSpec as P

ITERS = 3
LANES = 128
WIDTH = 512
VMEM = pl.BlockSpec(memory_space=pltpu.VMEM)
HBM = pl.BlockSpec(memory_space=pltpu.HBM)
LIMIT = 19 * 1024 * 1024


def params(limit=LIMIT):
    return pltpu.CompilerParams(vmem_limit_bytes=limit)


def lanes_of(ref, block):
    return ref[pl.ds(block * LANES, LANES), :].T


def spread_rows(vec, ref):
    for block in range(vec.shape[0]):
        row = jnp.broadcast_to(vec[block : block + 1, :], (LANES, LANES))
        ref[pl.ds(block * LANES, LANES), :] = row.T


def spread_cols(vec):
    return jnp.concatenate(
        [jnp.broadcast_to(vec[g : g + 1, :], (8, LANES)) for g in range(vec.shape[0])], axis=1
    )


def repeat_lanes(col, groups):
    return jnp.concatenate([col] * groups, axis=1)


def fold_lanes(x, op):
    parts = [x[:, g * LANES : (g + 1) * LANES] for g in range(x.shape[1] // LANES)]
    while len(parts) > 1:
        parts = [op(*parts[k : k + 2]) if k + 1 < len(parts) else parts[k] for k in range(0, len(parts), 2)]
    return parts[0]


def contract_last(left, right):
    return lax.dot_general(left, right, (((1,), (1,)), ((), ())), preferred_element_type=jnp.float32)


def text_copies(from_ref, to_ref, sems):
    chunks = [pl.ds(j * WIDTH, WIDTH) for j in range(to_ref.shape[0] // WIDTH)]
    copies = [pltpu.make_async_copy(from_ref.at[c], to_ref.at[c], sems.at[j]) for j, c in enumerate(chunks)]
    for copy in copies:
        copy.start()
    return copies


def multiply_chunk(j, audio_ref, text_ref, logits_ref, best_ref):
    step = 256
    at = pl.ds(j * WIDTH, WIDTH)

    def block(i, _):
        rows = pl.ds(pl.multiple_of(i * step, step), step)
        x = 10.0 * contract_last(audio_ref[rows, :], text_ref[at, :])
        logits_ref[rows, at] = x
        folded = fold_lanes(x, jnp.maximum)
        best_ref[rows, :] = folded if j == 0 else jnp.maximum(best_ref[rows, :], folded)
        return 0

    lax.fori_loop(0, audio_ref.shape[0] // step, block, 0)


def logits_kernel(audio_ref, text_hbm_ref, logits_ref, max_ref, text_ref, part_ref, sems):
    rows = logits_ref.shape[0]
    for j, copy in enumerate(text_copies(text_hbm_ref, text_ref, sems)):
        copy.wait()
        multiply_chunk(j, audio_ref, text_ref, logits_ref, part_ref)
    for b in range(rows // LANES):
        top = jnp.max(lanes_of(part_ref, b), axis=0, keepdims=True)
        for k in range(max_ref.shape[0]):
            max_ref[k, b : b + 1, :] = top


def teacher_logits(audio, text, peers):
    rows, columns = audio.shape[0], text.shape[0]
    return pl.pallas_call(
        logits_kernel,
        out_shape=(
            pltpu.VMEM((rows, columns), jnp.float32),
            jax.ShapeDtypeStruct((peers, rows // LANES, LANES), jnp.float32),
        ),
        in_specs=[VMEM, HBM],
        out_specs=(VMEM, VMEM),
        scratch_shapes=[
            pltpu.VMEM(text.shape, text.dtype),
            pltpu.VMEM((rows, LANES), jnp.float32),
            pltpu.SemaphoreType.DMA((columns // WIDTH,)),
        ],
        compiler_params=params(),
        name="logits",
    )(audio, streamed(text))


def put_columns(acc, sum_ref, out_ref):
    groups = sum_ref.shape[0]
    for g in range(groups):
        sum_ref[g : g + 1, :] = jnp.sum(acc[:, g * LANES : (g + 1) * LANES], axis=0, keepdims=True)
    total = sum_ref[...]
    for k in range(out_ref.shape[0]):
        out_ref[k] = total


def exp_kernel(max_ref, logits_ref, kernel_ref, out_ref, col_ref, sum_ref):
    rows, columns = logits_ref.shape
    spread_rows(jnp.max(max_ref[...], axis=0), col_ref)

    def step(i, acc):
        at = pl.ds(pl.multiple_of(i * 8, 8), 8)
        k = jnp.exp(logits_ref[at, :] - repeat_lanes(col_ref[at, :], columns // LANES))
        kernel_ref[at, :] = k
        return acc + k

    acc = lax.fori_loop(0, rows // 8, step, jnp.zeros((8, columns), jnp.float32), unroll=4)
    put_columns(acc, sum_ref, out_ref)


def exp_columns(maxima, logits, peers):
    rows, columns = logits.shape
    return pl.pallas_call(
        exp_kernel,
        out_shape=(
            pltpu.VMEM((rows, columns), jnp.float32),
            jax.ShapeDtypeStruct((peers, columns // LANES, LANES), jnp.float32),
        ),
        in_specs=[VMEM, VMEM],
        out_specs=(VMEM, VMEM),
        scratch_shapes=[
            pltpu.VMEM((rows, LANES), jnp.float32),
            pltpu.VMEM((columns // LANES, LANES), jnp.float32),
        ],
        input_output_aliases={1: 0},
        compiler_params=params(),
        name="exp_columns",
    )(maxima, resident(logits))


def row_kernel(parts_ref, kernel_ref, stat_ref, out_ref, scale_ref, part_ref):
    if stat_ref is not None:
        kernel_ref = kernel_ref.at[0]
    rows = kernel_ref.shape[0]
    blocks = rows // LANES
    scale_ref[...] = 1.0 / jnp.sum(parts_ref[...], axis=0)
    scale = spread_cols(scale_ref[...])

    def step(i, _):
        at = pl.ds(pl.multiple_of(i * 8, 8), 8)
        part_ref[at, :] = fold_lanes(kernel_ref[at, :] * scale, jnp.add)
        return 0

    lax.fori_loop(0, rows // 8, step, 0, unroll=4)
    for b in range(blocks):
        total = jnp.sum(lanes_of(part_ref, b), axis=0, keepdims=True)
        for k in range(out_ref.shape[0]):
            out_ref[k, b : b + 1, :] = total
    if stat_ref is not None:
        for k in range(out_ref.shape[0]):
            out_ref[k, blocks:, :] = stat_ref[...]


def row_sums(parts, kernel, peers, stats=None):
    rows, columns = kernel.shape[-2:]
    if stats is None:
        extra, body = (), lambda parts_ref, kernel_ref, *refs: row_kernel(parts_ref, kernel_ref, None, *refs)
    else:
        extra, body = (stats,), row_kernel
    return pl.pallas_call(
        body,
        out_shape=(
            jax.ShapeDtypeStruct((peers, rows // LANES * (3 if extra else 1), LANES), jnp.float32),
            jax.ShapeDtypeStruct((columns // LANES, LANES), jnp.float32),
        ),
        in_specs=[VMEM] * (2 + len(extra)),
        out_specs=(VMEM, VMEM),
        scratch_shapes=[pltpu.VMEM((rows, LANES), jnp.float32)],
        compiler_params=params(),
        name="row_sums",
    )(parts, resident(kernel), *extra)


def column_kernel(parts_ref, kernel_ref, out_ref, col_ref, sum_ref):
    rows, columns = kernel_ref.shape
    spread_rows(1.0 / jnp.sum(parts_ref[...], axis=0), col_ref)

    def step(i, acc):
        at = pl.ds(pl.multiple_of(i * 8, 8), 8)
        return acc + kernel_ref[at, :] * repeat_lanes(col_ref[at, :], columns // LANES)

    acc = lax.fori_loop(0, rows // 8, step, jnp.zeros((8, columns), jnp.float32), unroll=4)
    put_columns(acc, sum_ref, out_ref)


def column_sums(parts, kernel, peers):
    rows, columns = kernel.shape
    return pl.pallas_call(
        column_kernel,
        out_shape=jax.ShapeDtypeStruct((peers, columns // LANES, LANES), jnp.float32),
        in_specs=[VMEM, VMEM],
        out_specs=VMEM,
        scratch_shapes=[
            pltpu.VMEM((rows, LANES), jnp.float32),
            pltpu.VMEM((columns // LANES, LANES), jnp.float32),
        ],
        compiler_params=params(),
        name="column_sums",
    )(parts, resident(kernel))


def student_kernel(
    audio_ref, text_hbm_ref, kernel_hbm_ref, pair_ref, stat_ref, text_ref, part_ref, sems, kernel_sem
):
    kernel_ref, exp_ref = pair_ref.at[0], pair_ref.at[1]
    rows, columns = exp_ref.shape
    blocks = rows // LANES
    kernel_copy = pltpu.make_async_copy(kernel_hbm_ref, kernel_ref, kernel_sem)
    for j, copy in enumerate(text_copies(text_hbm_ref, text_ref, sems)):
        copy.wait()
        if j == 0:
            kernel_copy.start()
        multiply_chunk(j, audio_ref, text_ref, exp_ref, part_ref)
    for b in range(blocks):
        top = jnp.max(lanes_of(part_ref, b), axis=0, keepdims=True)
        stat_ref[b : b + 1, :] = top
        part_ref[pl.ds(b * LANES, LANES), :] = jnp.broadcast_to(top, (LANES, LANES)).T

    def step(i, _):
        at = pl.ds(pl.multiple_of(i * 8, 8), 8)
        e = jnp.exp(exp_ref[at, :] - repeat_lanes(part_ref[at, :], columns // LANES))
        exp_ref[at, :] = e
        part_ref[at, :] = fold_lanes(e, jnp.add)
        return 0

    lax.fori_loop(0, rows // 8, step, 0, unroll=4)
    for b in range(blocks):
        total = jnp.sum(lanes_of(part_ref, b), axis=0, keepdims=True)
        stat_ref[blocks + b : blocks + b + 1, :] = total
    kernel_copy.wait()


def student_softmax(audio, text, kernel):
    rows, columns = audio.shape[0], text.shape[0]
    return pl.pallas_call(
        student_kernel,
        out_shape=(
            pltpu.VMEM((2, rows, columns), jnp.float32),
            jax.ShapeDtypeStruct((2 * (rows // LANES), LANES), jnp.float32),
        ),
        in_specs=[VMEM, HBM, HBM],
        out_specs=(VMEM, VMEM),
        scratch_shapes=[
            pltpu.VMEM(text.shape, text.dtype),
            pltpu.VMEM((rows, LANES), jnp.float32),
            pltpu.SemaphoreType.DMA((columns // WIDTH,)),
            pltpu.SemaphoreType.DMA,
        ],
        compiler_params=params(),
        name="student_softmax",
    )(audio, streamed(text), streamed(kernel))


def residual_kernel(
    rows_ref, scale_ref, own_ref, pair_ref, audio_hbm_ref, text_hbm_ref,
    audio_out_ref, text_out_ref, weight_ref, prob_ref, residual_ref, audio_ref, text_ref, audio_sem, text_sem,
):
    kernel_ref, exp_ref = pair_ref.at[0], pair_ref.at[1]
    step, depth = audio_out_ref.shape
    rows, columns = pair_ref.shape[1:]
    blocks = own_ref.shape[0] // 2
    groups = WIDTH // LANES
    i = pl.program_id(0)
    audio_copy = pltpu.make_async_copy(audio_hbm_ref, audio_ref, audio_sem)
    text_copy = pltpu.make_async_copy(text_hbm_ref, text_ref, text_sem)

    @pl.when(i == 0)
    def _():
        text_copy.start()
        audio_copy.start()
        spread_rows(1.0 / jnp.sum(rows_ref[:, :blocks, :], axis=0), weight_ref)
        tops = rows_ref[:, blocks : 2 * blocks, :]
        top = jnp.max(tops, axis=0)
        total = jnp.sum(jnp.exp(tops - top[None]) * rows_ref[:, 2 * blocks :, :], axis=0)
        spread_rows(jnp.exp(own_ref[:blocks, :] - top) / total, prob_ref)

    at = pl.ds(pl.multiple_of(i * step, step), step)
    for j in range(columns // WIDTH):
        lanes = pl.ds(j * WIDTH, WIDTH)
        scale = spread_cols(scale_ref[j * groups : (j + 1) * groups, :])
        scale = jnp.concatenate([scale] * (step // 8), axis=0)
        target = (repeat_lanes(weight_ref[at, :], groups) * kernel_ref[at, lanes]) * scale
        prob = exp_ref[at, lanes] * repeat_lanes(prob_ref[at, :], groups)
        residual_ref[at, lanes] = (prob - target).astype(jnp.bfloat16)
    pl.when(i == 0)(text_copy.wait)
    audio_out_ref[...] = 10.0 * jnp.dot(residual_ref[at, :], text_ref[...], preferred_element_type=jnp.float32)

    @pl.when(i == pl.num_programs(0) - 1)
    def _():
        audio_copy.wait()
        for j in range(columns // WIDTH):
            grad = lax.dot_general(
                residual_ref[:, pl.ds(j * WIDTH, WIDTH)],
                audio_ref[...],
                (((0,), (0,)), ((), ())),
                preferred_element_type=jnp.float32,
            )
            text_out_ref[pl.ds(j * WIDTH, WIDTH), :] = (10.0 * grad).astype(text_out_ref.dtype)


def residual_grads(row_parts, scale, own, pair, audio, text, dtype):
    rows, columns = pair.shape[1:]
    depth = audio.shape[1]
    step = 256
    return pl.pallas_call(
        residual_kernel,
        grid=(rows // step,),
        out_shape=(
            jax.ShapeDtypeStruct((rows, depth), jnp.float32),
            pltpu.VMEM((columns, depth), dtype),
        ),
        in_specs=[VMEM] * 4 + [HBM] * 2,
        out_specs=(pl.BlockSpec((step, depth), lambda i: (i, 0)), VMEM),
        scratch_shapes=[
            pltpu.VMEM((rows, LANES), jnp.float32),
            pltpu.VMEM((rows, LANES), jnp.float32),
            pltpu.VMEM((rows, columns), jnp.bfloat16),
            pltpu.VMEM(audio.shape, audio.dtype),
            pltpu.VMEM(text.shape, text.dtype),
            pltpu.SemaphoreType.DMA,
            pltpu.SemaphoreType.DMA,
        ],
        compiler_params=params(),
        name="residual_grads",
    )(row_parts, scale, own, resident(pair), streamed(audio), streamed(text))


def resident(x):
    return pltpu.with_memory_space_constraint(x, pltpu.VMEM)


def streamed(x):
    return pltpu.with_memory_space_constraint(x, pltpu.HBM)


def gather_a2a(x, axis, n):
    spread = jnp.broadcast_to(x[None], (n, *x.shape))
    return lax.all_to_all(spread, axis, 0, 0).reshape(n * x.shape[0], x.shape[1])


def swap(x, axis):
    return lax.all_to_all(x, axis, 0, 0)


def body(clips, caps, teacher_audio, teacher_text, student_audio, student_text):
    text_t = lax.all_gather(teacher_text, "clip", axis=0, tiled=True)
    audio_t = gather_a2a(teacher_audio, "cap", caps)
    student_audio, student_text, audio_t = lax.optimization_barrier((student_audio, student_text, audio_t))
    audio_s = gather_a2a(student_audio, "cap", caps)
    audio_s, text_t = lax.optimization_barrier((audio_s, text_t))
    text_s = lax.all_gather(student_text, "clip", axis=0, tiled=True)
    logits, maxima = teacher_logits(audio_t, text_t, caps)
    kernel, columns = exp_columns(swap(maxima, "cap"), logits, clips)
    for _ in range(ITERS - 1):
        row_parts, _ = row_sums(swap(columns, "clip"), kernel, caps)
        columns = column_sums(swap(row_parts, "cap"), kernel, clips)
    columns, text_s = lax.optimization_barrier((columns, text_s))
    columns, audio_s = lax.optimization_barrier((swap(columns, "clip"), audio_s))
    pair, stats = student_softmax(audio_s, text_s, kernel)
    row_parts, scale = row_sums(columns, pair, caps, stats)
    row_parts = swap(row_parts, "cap")
    audio_part, text_part = residual_grads(
        row_parts, scale, stats, pair, audio_s, text_s, jnp.bfloat16
    )
    audio_grad = lax.psum_scatter(audio_part, "cap", scatter_dimension=0, tiled=True)
    text_parts = swap(text_part.reshape(clips, -1, text_part.shape[1]), "clip")
    text_grad = jnp.sum(text_parts.astype(jnp.float32), axis=0)
    return audio_grad, text_grad


def solution(mesh):
    placed = (
        P(("clip", "cap"), None),
        P(("cap", "clip"), None),
        P(("clip", "cap"), None),
        P(("cap", "clip"), None),
    )
    return jax.shard_map(
        functools.partial(body, mesh.shape["clip"], mesh.shape["cap"]),
        mesh=mesh,
        in_specs=placed,
        out_specs=(P(("clip", "cap"), None), P(("cap", "clip"), None)),
        check_vma=False,
    )
```

```python
import functools

import jax
import jax.numpy as jnp
from jax import lax
from jax.experimental import pallas as pl
from jax.experimental.pallas import tpu as pltpu
from jax.sharding import PartitionSpec as P

ITERS = 3
LANES = 128
WIDTH = 512
VMEM = pl.BlockSpec(memory_space=pltpu.VMEM)
HBM = pl.BlockSpec(memory_space=pltpu.HBM)
LIMIT = 19 * 1024 * 1024


def params(limit=LIMIT):
    return pltpu.CompilerParams(vmem_limit_bytes=limit)


def lanes_of(ref, block):
    return ref[pl.ds(block * LANES, LANES), :].T


def spread_rows(vec, ref):
    for block in range(vec.shape[0]):
        row = jnp.broadcast_to(vec[block : block + 1, :], (LANES, LANES))
        ref[pl.ds(block * LANES, LANES), :] = row.T


def spread_cols(vec):
    return jnp.concatenate(
        [jnp.broadcast_to(vec[g : g + 1, :], (8, LANES)) for g in range(vec.shape[0])], axis=1
    )


def repeat_lanes(col, groups):
    return jnp.concatenate([col] * groups, axis=1)


def fold_lanes(x, op):
    parts = [x[:, g * LANES : (g + 1) * LANES] for g in range(x.shape[1] // LANES)]
    while len(parts) > 1:
        parts = [op(*parts[k : k + 2]) if k + 1 < len(parts) else parts[k] for k in range(0, len(parts), 2)]
    return parts[0]


def contract_last(left, right):
    return lax.dot_general(left, right, (((1,), (1,)), ((), ())), preferred_element_type=jnp.float32)


def text_copies(from_ref, to_ref, sems):
    chunks = [pl.ds(j * WIDTH, WIDTH) for j in range(to_ref.shape[0] // WIDTH)]
    copies = [pltpu.make_async_copy(from_ref.at[c], to_ref.at[c], sems.at[j]) for j, c in enumerate(chunks)]
    for copy in copies:
        copy.start()
    return copies


def multiply_rows(audio_ref, text_ref, logits_ref, best_ref, copies, after_first):
    step = 256

    def block(i, waits):
        rows = pl.ds(pl.multiple_of(i * step, step), step)
        left = audio_ref[rows, :]
        best = None
        for j, copy in enumerate(copies):
            if waits:
                copy.wait()
            at = pl.ds(j * WIDTH, WIDTH)
            x = 10.0 * contract_last(left, text_ref[at, :])
            logits_ref[rows, at] = x
            folded = fold_lanes(x, jnp.maximum)
            best = folded if best is None else jnp.maximum(best, folded)
        best_ref[rows, :] = best
        return 0

    block(0, True)
    after_first()
    lax.fori_loop(1, audio_ref.shape[0] // step, lambda i, _: block(i, False), 0)


def logits_kernel(audio_ref, text_hbm_ref, logits_ref, max_ref, text_ref, part_ref, sems):
    rows = logits_ref.shape[0]
    copies = text_copies(text_hbm_ref, text_ref, sems)
    multiply_rows(audio_ref, text_ref, logits_ref, part_ref, copies, lambda: None)
    for b in range(rows // LANES):
        top = jnp.max(lanes_of(part_ref, b), axis=0, keepdims=True)
        for k in range(max_ref.shape[0]):
            max_ref[k, b : b + 1, :] = top


def teacher_logits(audio, text, peers):
    rows, columns = audio.shape[0], text.shape[0]
    return pl.pallas_call(
        logits_kernel,
        out_shape=(
            pltpu.VMEM((rows, columns), jnp.float32),
            jax.ShapeDtypeStruct((peers, rows // LANES, LANES), jnp.float32),
        ),
        in_specs=[VMEM, HBM],
        out_specs=(VMEM, VMEM),
        scratch_shapes=[
            pltpu.VMEM(text.shape, text.dtype),
            pltpu.VMEM((rows, LANES), jnp.float32),
            pltpu.SemaphoreType.DMA((columns // WIDTH,)),
        ],
        compiler_params=params(),
        name="logits",
    )(audio, streamed(text))


def put_columns(acc, sum_ref, out_ref):
    groups = sum_ref.shape[0]
    for g in range(groups):
        sum_ref[g : g + 1, :] = jnp.sum(acc[:, g * LANES : (g + 1) * LANES], axis=0, keepdims=True)
    total = sum_ref[...]
    for k in range(out_ref.shape[0]):
        out_ref[k] = total


def exp_kernel(max_ref, logits_ref, kernel_ref, out_ref, col_ref, sum_ref):
    rows, columns = logits_ref.shape
    spread_rows(jnp.max(max_ref[...], axis=0), col_ref)

    def step(i, acc):
        at = pl.ds(pl.multiple_of(i * 8, 8), 8)
        k = jnp.exp(logits_ref[at, :] - repeat_lanes(col_ref[at, :], columns // LANES))
        kernel_ref[at, :] = k
        return acc + k

    acc = lax.fori_loop(0, rows // 8, step, jnp.zeros((8, columns), jnp.float32), unroll=4)
    put_columns(acc, sum_ref, out_ref)


def exp_columns(maxima, logits, peers):
    rows, columns = logits.shape
    return pl.pallas_call(
        exp_kernel,
        out_shape=(
            pltpu.VMEM((rows, columns), jnp.float32),
            jax.ShapeDtypeStruct((peers, columns // LANES, LANES), jnp.float32),
        ),
        in_specs=[VMEM, VMEM],
        out_specs=(VMEM, VMEM),
        scratch_shapes=[
            pltpu.VMEM((rows, LANES), jnp.float32),
            pltpu.VMEM((columns // LANES, LANES), jnp.float32),
        ],
        input_output_aliases={1: 0},
        compiler_params=params(),
        name="exp_columns",
    )(maxima, resident(logits))


def row_kernel(parts_ref, kernel_ref, stat_ref, out_ref, scale_ref, part_ref):
    if stat_ref is not None:
        kernel_ref = kernel_ref.at[0]
    rows = kernel_ref.shape[0]
    blocks = rows // LANES
    scale_ref[...] = 1.0 / jnp.sum(parts_ref[...], axis=0)
    scale = spread_cols(scale_ref[...])

    def step(i, _):
        at = pl.ds(pl.multiple_of(i * 8, 8), 8)
        part_ref[at, :] = fold_lanes(kernel_ref[at, :] * scale, jnp.add)
        return 0

    lax.fori_loop(0, rows // 8, step, 0, unroll=4)
    for b in range(blocks):
        total = jnp.sum(lanes_of(part_ref, b), axis=0, keepdims=True)
        for k in range(out_ref.shape[0]):
            out_ref[k, b : b + 1, :] = total
    if stat_ref is not None:
        for k in range(out_ref.shape[0]):
            out_ref[k, blocks:, :] = stat_ref[...]


def row_sums(parts, kernel, peers, stats=None):
    rows, columns = kernel.shape[-2:]
    if stats is None:
        extra, body = (), lambda parts_ref, kernel_ref, *refs: row_kernel(parts_ref, kernel_ref, None, *refs)
    else:
        extra, body = (stats,), row_kernel
    return pl.pallas_call(
        body,
        out_shape=(
            jax.ShapeDtypeStruct((peers, rows // LANES * (3 if extra else 1), LANES), jnp.float32),
            jax.ShapeDtypeStruct((columns // LANES, LANES), jnp.float32),
        ),
        in_specs=[VMEM] * (2 + len(extra)),
        out_specs=(VMEM, VMEM),
        scratch_shapes=[pltpu.VMEM((rows, LANES), jnp.float32)],
        compiler_params=params(),
        name="row_sums",
    )(parts, resident(kernel), *extra)


def column_kernel(parts_ref, kernel_ref, out_ref, col_ref, sum_ref):
    rows, columns = kernel_ref.shape
    spread_rows(1.0 / jnp.sum(parts_ref[...], axis=0), col_ref)

    def step(i, acc):
        at = pl.ds(pl.multiple_of(i * 8, 8), 8)
        return acc + kernel_ref[at, :] * repeat_lanes(col_ref[at, :], columns // LANES)

    acc = lax.fori_loop(0, rows // 8, step, jnp.zeros((8, columns), jnp.float32), unroll=4)
    put_columns(acc, sum_ref, out_ref)


def column_sums(parts, kernel, peers):
    rows, columns = kernel.shape
    return pl.pallas_call(
        column_kernel,
        out_shape=jax.ShapeDtypeStruct((peers, columns // LANES, LANES), jnp.float32),
        in_specs=[VMEM, VMEM],
        out_specs=VMEM,
        scratch_shapes=[
            pltpu.VMEM((rows, LANES), jnp.float32),
            pltpu.VMEM((columns // LANES, LANES), jnp.float32),
        ],
        compiler_params=params(),
        name="column_sums",
    )(parts, resident(kernel))


def student_kernel(
    audio_ref, text_hbm_ref, kernel_hbm_ref, pair_ref, stat_ref, text_ref, part_ref, sems, kernel_sem
):
    kernel_ref, exp_ref = pair_ref.at[0], pair_ref.at[1]
    rows, columns = exp_ref.shape
    blocks = rows // LANES
    kernel_copy = pltpu.make_async_copy(kernel_hbm_ref, kernel_ref, kernel_sem)
    copies = text_copies(text_hbm_ref, text_ref, sems)
    multiply_rows(audio_ref, text_ref, exp_ref, part_ref, copies, kernel_copy.start)
    for b in range(blocks):
        top = jnp.max(lanes_of(part_ref, b), axis=0, keepdims=True)
        stat_ref[b : b + 1, :] = top
        part_ref[pl.ds(b * LANES, LANES), :] = jnp.broadcast_to(top, (LANES, LANES)).T

    def step(i, _):
        at = pl.ds(pl.multiple_of(i * 8, 8), 8)
        e = jnp.exp(exp_ref[at, :] - repeat_lanes(part_ref[at, :], columns // LANES))
        exp_ref[at, :] = e
        part_ref[at, :] = fold_lanes(e, jnp.add)
        return 0

    lax.fori_loop(0, rows // 8, step, 0, unroll=4)
    for b in range(blocks):
        total = jnp.sum(lanes_of(part_ref, b), axis=0, keepdims=True)
        stat_ref[blocks + b : blocks + b + 1, :] = total
    kernel_copy.wait()


def student_softmax(audio, text, kernel):
    rows, columns = audio.shape[0], text.shape[0]
    return pl.pallas_call(
        student_kernel,
        out_shape=(
            pltpu.VMEM((2, rows, columns), jnp.float32),
            jax.ShapeDtypeStruct((2 * (rows // LANES), LANES), jnp.float32),
        ),
        in_specs=[VMEM, HBM, HBM],
        out_specs=(VMEM, VMEM),
        scratch_shapes=[
            pltpu.VMEM(text.shape, text.dtype),
            pltpu.VMEM((rows, LANES), jnp.float32),
            pltpu.SemaphoreType.DMA((columns // WIDTH,)),
            pltpu.SemaphoreType.DMA,
        ],
        compiler_params=params(),
        name="student_softmax",
    )(audio, streamed(text), streamed(kernel))


def residual_kernel(
    rows_ref, scale_ref, own_ref, pair_ref, audio_ref, text_ref,
    audio_out_ref, text_out_ref, weight_ref, prob_ref, residual_ref,
):
    kernel_ref, exp_ref = pair_ref.at[0], pair_ref.at[1]
    step, depth = audio_out_ref.shape
    rows, columns = pair_ref.shape[1:]
    blocks = own_ref.shape[0] // 2
    groups = WIDTH // LANES
    i = pl.program_id(0)

    @pl.when(i == 0)
    def _():
        spread_rows(1.0 / jnp.sum(rows_ref[:, :blocks, :], axis=0), weight_ref)
        tops = rows_ref[:, blocks : 2 * blocks, :]
        top = jnp.max(tops, axis=0)
        total = jnp.sum(jnp.exp(tops - top[None]) * rows_ref[:, 2 * blocks :, :], axis=0)
        spread_rows(jnp.exp(own_ref[:blocks, :] - top) / total, prob_ref)

    at = pl.ds(pl.multiple_of(i * step, step), step)
    for j in range(columns // WIDTH):
        lanes = pl.ds(j * WIDTH, WIDTH)
        scale = spread_cols(scale_ref[j * groups : (j + 1) * groups, :])
        scale = jnp.concatenate([scale] * (step // 8), axis=0)
        target = (repeat_lanes(weight_ref[at, :], groups) * kernel_ref[at, lanes]) * scale
        prob = exp_ref[at, lanes] * repeat_lanes(prob_ref[at, :], groups)
        residual_ref[at, lanes] = (prob - target).astype(jnp.bfloat16)
    audio_out_ref[...] = 10.0 * jnp.dot(residual_ref[at, :], text_ref[...], preferred_element_type=jnp.float32)

    @pl.when(i == pl.num_programs(0) - 1)
    def _():
        for j in range(columns // WIDTH):
            grad = lax.dot_general(
                residual_ref[:, pl.ds(j * WIDTH, WIDTH)],
                audio_ref[...],
                (((0,), (0,)), ((), ())),
                preferred_element_type=jnp.float32,
            )
            text_out_ref[pl.ds(j * WIDTH, WIDTH), :] = (10.0 * grad).astype(text_out_ref.dtype)


def residual_grads(row_parts, scale, own, pair, audio, text, dtype):
    rows, columns = pair.shape[1:]
    depth = audio.shape[1]
    step = 256
    return pl.pallas_call(
        residual_kernel,
        grid=(rows // step,),
        out_shape=(
            jax.ShapeDtypeStruct((rows, depth), jnp.float32),
            pltpu.VMEM((columns, depth), dtype),
        ),
        in_specs=[VMEM] * 6,
        out_specs=(pl.BlockSpec((step, depth), lambda i: (i, 0)), VMEM),
        scratch_shapes=[
            pltpu.VMEM((rows, LANES), jnp.float32),
            pltpu.VMEM((rows, LANES), jnp.float32),
            pltpu.VMEM((rows, columns), jnp.bfloat16),
        ],
        compiler_params=params(),
        name="residual_grads",
    )(row_parts, scale, own, resident(pair), audio, text)


def resident(x):
    return pltpu.with_memory_space_constraint(x, pltpu.VMEM)


def streamed(x):
    return pltpu.with_memory_space_constraint(x, pltpu.HBM)


def gather_a2a(x, axis, n):
    spread = jnp.broadcast_to(x[None], (n, *x.shape))
    return lax.all_to_all(spread, axis, 0, 0).reshape(n * x.shape[0], x.shape[1])


def swap(x, axis):
    return lax.all_to_all(x, axis, 0, 0)


def body(clips, caps, teacher_audio, teacher_text, student_audio, student_text):
    text_t = lax.all_gather(teacher_text, "clip", axis=0, tiled=True)
    audio_t = gather_a2a(teacher_audio, "cap", caps)
    student_audio, student_text, audio_t = lax.optimization_barrier((student_audio, student_text, audio_t))
    audio_s = gather_a2a(student_audio, "cap", caps)
    audio_s, text_t = lax.optimization_barrier((audio_s, text_t))
    text_s = lax.all_gather(student_text, "clip", axis=0, tiled=True)
    logits, maxima = teacher_logits(audio_t, text_t, caps)
    kernel, columns = exp_columns(swap(maxima, "cap"), logits, clips)
    for _ in range(ITERS - 1):
        row_parts, _ = row_sums(swap(columns, "clip"), kernel, caps)
        columns = column_sums(swap(row_parts, "cap"), kernel, clips)
    columns, text_s = lax.optimization_barrier((columns, text_s))
    columns, audio_s = lax.optimization_barrier((swap(columns, "clip"), audio_s))
    pair, stats = student_softmax(audio_s, text_s, kernel)
    row_parts, scale = row_sums(columns, pair, caps, stats)
    row_parts = swap(row_parts, "cap")
    audio_part, text_part = residual_grads(
        row_parts, scale, stats, pair, audio_s, text_s, jnp.bfloat16
    )
    audio_grad = lax.psum_scatter(audio_part, "cap", scatter_dimension=0, tiled=True)
    text_parts = swap(text_part.reshape(clips, -1, text_part.shape[1]), "clip")
    text_grad = jnp.sum(text_parts.astype(jnp.float32), axis=0)
    return audio_grad, text_grad


def solution(mesh):
    placed = (
        P(("clip", "cap"), None),
        P(("cap", "clip"), None),
        P(("clip", "cap"), None),
        P(("cap", "clip"), None),
    )
    return jax.shard_map(
        functools.partial(body, mesh.shape["clip"], mesh.shape["cap"]),
        mesh=mesh,
        in_specs=placed,
        out_specs=(P(("clip", "cap"), None), P(("cap", "clip"), None)),
        check_vma=False,
    )
```

```python
import functools

import jax
import jax.numpy as jnp
from jax import lax
from jax.experimental import pallas as pl
from jax.experimental.pallas import tpu as pltpu
from jax.sharding import PartitionSpec as P

ITERS = 3
LANES = 128
WIDTH = 512
VMEM = pl.BlockSpec(memory_space=pltpu.VMEM)
LIMIT = 19 * 1024 * 1024


def params(limit=LIMIT):
    return pltpu.CompilerParams(vmem_limit_bytes=limit)


def lanes_of(ref, block):
    return ref[pl.ds(block * LANES, LANES), :].T


def spread_rows(vec, ref):
    for block in range(vec.shape[0]):
        row = jnp.broadcast_to(vec[block : block + 1, :], (LANES, LANES))
        ref[pl.ds(block * LANES, LANES), :] = row.T


def spread_cols(vec):
    return jnp.concatenate(
        [jnp.broadcast_to(vec[g : g + 1, :], (8, LANES)) for g in range(vec.shape[0])], axis=1
    )


def repeat_lanes(col, groups):
    return jnp.concatenate([col] * groups, axis=1)


def fold_lanes(x, op):
    parts = [x[:, g * LANES : (g + 1) * LANES] for g in range(x.shape[1] // LANES)]
    while len(parts) > 1:
        parts = [op(*parts[k : k + 2]) if k + 1 < len(parts) else parts[k] for k in range(0, len(parts), 2)]
    return parts[0]


def contract_last(left, right):
    return lax.dot_general(left, right, (((1,), (1,)), ((), ())), preferred_element_type=jnp.float32)


def logits_kernel(audio_ref, text_ref, probe_ref, logits_ref, max_ref, part_ref):
    rows, columns = logits_ref.shape
    step = 256

    def block(i, _):
        base = pl.multiple_of(i * step, step)
        left = audio_ref[pl.ds(base, step), :]
        best = None
        for j in range(columns // WIDTH):
            at = j * WIDTH
            x = 10.0 * contract_last(left, text_ref[pl.ds(at, WIDTH), :])
            logits_ref[pl.ds(base, step), pl.ds(at, WIDTH)] = x
            folded = fold_lanes(x, jnp.maximum)
            best = folded if best is None else jnp.maximum(best, folded)
        part_ref[pl.ds(base, step), :] = best
        return 0

    lax.fori_loop(0, rows // step, block, 0)
    for b in range(rows // LANES):
        top = jnp.max(lanes_of(part_ref, b), axis=0, keepdims=True)
        for k in range(max_ref.shape[0]):
            max_ref[k, b : b + 1, :] = top


def teacher_logits(audio, text, probe, peers):
    rows, columns = audio.shape[0], text.shape[0]
    return pl.pallas_call(
        logits_kernel,
        out_shape=(
            pltpu.VMEM((rows, columns), jnp.float32),
            jax.ShapeDtypeStruct((peers, rows // LANES, LANES), jnp.float32),
        ),
        in_specs=[VMEM, VMEM, VMEM],
        out_specs=(VMEM, VMEM),
        scratch_shapes=[pltpu.VMEM((rows, LANES), jnp.float32)],
        compiler_params=params(),
        name="logits",
    )(audio, text, probe)


def put_columns(acc, sum_ref, out_ref):
    groups = sum_ref.shape[0]
    for g in range(groups):
        sum_ref[g : g + 1, :] = jnp.sum(acc[:, g * LANES : (g + 1) * LANES], axis=0, keepdims=True)
    total = sum_ref[...]
    for k in range(out_ref.shape[0]):
        out_ref[k] = total


def exp_kernel(max_ref, logits_ref, kernel_ref, out_ref, col_ref, sum_ref):
    rows, columns = logits_ref.shape
    spread_rows(jnp.max(max_ref[...], axis=0), col_ref)

    def step(i, acc):
        at = pl.ds(pl.multiple_of(i * 8, 8), 8)
        k = jnp.exp(logits_ref[at, :] - repeat_lanes(col_ref[at, :], columns // LANES))
        kernel_ref[at, :] = k
        return acc + k

    acc = lax.fori_loop(0, rows // 8, step, jnp.zeros((8, columns), jnp.float32), unroll=4)
    put_columns(acc, sum_ref, out_ref)


def exp_columns(maxima, logits, peers):
    rows, columns = logits.shape
    return pl.pallas_call(
        exp_kernel,
        out_shape=(
            pltpu.VMEM((rows, columns), jnp.float32),
            jax.ShapeDtypeStruct((peers, columns // LANES, LANES), jnp.float32),
        ),
        in_specs=[VMEM, VMEM],
        out_specs=(VMEM, VMEM),
        scratch_shapes=[
            pltpu.VMEM((rows, LANES), jnp.float32),
            pltpu.VMEM((columns // LANES, LANES), jnp.float32),
        ],
        input_output_aliases={1: 0},
        compiler_params=params(),
        name="exp_columns",
    )(maxima, resident(logits))


def row_kernel(parts_ref, kernel_ref, stat_ref, out_ref, scale_ref, part_ref):
    if stat_ref is not None:
        kernel_ref = kernel_ref.at[0]
    rows = kernel_ref.shape[0]
    blocks = rows // LANES
    scale_ref[...] = 1.0 / jnp.sum(parts_ref[...], axis=0)
    scale = spread_cols(scale_ref[...])

    def step(i, _):
        at = pl.ds(pl.multiple_of(i * 8, 8), 8)
        part_ref[at, :] = fold_lanes(kernel_ref[at, :] * scale, jnp.add)
        return 0

    lax.fori_loop(0, rows // 8, step, 0, unroll=4)
    for b in range(blocks):
        total = jnp.sum(lanes_of(part_ref, b), axis=0, keepdims=True)
        for k in range(out_ref.shape[0]):
            out_ref[k, b : b + 1, :] = total
    if stat_ref is not None:
        for k in range(out_ref.shape[0]):
            out_ref[k, blocks:, :] = stat_ref[...]


def row_sums(parts, kernel, peers, stats=None):
    rows, columns = kernel.shape[-2:]
    if stats is None:
        extra, body = (), lambda parts_ref, kernel_ref, *refs: row_kernel(parts_ref, kernel_ref, None, *refs)
    else:
        extra, body = (stats,), row_kernel
    return pl.pallas_call(
        body,
        out_shape=(
            jax.ShapeDtypeStruct((peers, rows // LANES * (3 if extra else 1), LANES), jnp.float32),
            jax.ShapeDtypeStruct((columns // LANES, LANES), jnp.float32),
        ),
        in_specs=[VMEM] * (2 + len(extra)),
        out_specs=(VMEM, VMEM),
        scratch_shapes=[pltpu.VMEM((rows, LANES), jnp.float32)],
        compiler_params=params(),
        name="row_sums",
    )(parts, resident(kernel), *extra)


def column_kernel(parts_ref, kernel_ref, out_ref, col_ref, sum_ref):
    rows, columns = kernel_ref.shape
    spread_rows(1.0 / jnp.sum(parts_ref[...], axis=0), col_ref)

    def step(i, acc):
        at = pl.ds(pl.multiple_of(i * 8, 8), 8)
        return acc + kernel_ref[at, :] * repeat_lanes(col_ref[at, :], columns // LANES)

    acc = lax.fori_loop(0, rows // 8, step, jnp.zeros((8, columns), jnp.float32), unroll=4)
    put_columns(acc, sum_ref, out_ref)


def column_sums(parts, kernel, peers):
    rows, columns = kernel.shape
    return pl.pallas_call(
        column_kernel,
        out_shape=jax.ShapeDtypeStruct((peers, columns // LANES, LANES), jnp.float32),
        in_specs=[VMEM, VMEM],
        out_specs=VMEM,
        scratch_shapes=[
            pltpu.VMEM((rows, LANES), jnp.float32),
            pltpu.VMEM((columns // LANES, LANES), jnp.float32),
        ],
        compiler_params=params(),
        name="column_sums",
    )(parts, resident(kernel))


def student_kernel(audio_ref, text_hbm_ref, kernel_hbm_ref, pair_ref, stat_ref, text_ref, text_sem, kernel_sem):
    kernel_ref, exp_ref = pair_ref.at[0], pair_ref.at[1]
    rows, columns = pair_ref.shape[1:]
    text_copy = pltpu.make_async_copy(text_hbm_ref, text_ref, text_sem)
    kernel_copy = pltpu.make_async_copy(kernel_hbm_ref, kernel_ref, kernel_sem)
    text_copy.start()
    text_copy.wait()
    kernel_copy.start()
    step = 256
    here = step // LANES
    blocks = rows // LANES

    def block(i, _):
        base = pl.multiple_of(i * step, step)
        left = audio_ref[pl.ds(base, step), :]
        best = None
        for j in range(columns // WIDTH):
            x = 10.0 * contract_last(left, text_ref[pl.ds(j * WIDTH, WIDTH), :])
            exp_ref[pl.ds(base, step), pl.ds(j * WIDTH, WIDTH)] = x
            folded = fold_lanes(x, jnp.maximum)
            best = folded if best is None else jnp.maximum(best, folded)
        for b in range(here):
            at = pl.ds(pl.multiple_of(base + b * LANES, LANES), LANES)
            top = jnp.max(best[b * LANES : (b + 1) * LANES, :].T, axis=0, keepdims=True)
            stat_ref[pl.ds(i * here + b, 1), :] = top
            top = repeat_lanes(jnp.broadcast_to(top, (LANES, LANES)).T, WIDTH // LANES)
            total = None
            for j in range(columns // WIDTH):
                e = jnp.exp(exp_ref[at, pl.ds(j * WIDTH, WIDTH)] - top)
                exp_ref[at, pl.ds(j * WIDTH, WIDTH)] = e
                folded = fold_lanes(e, jnp.add)
                total = folded if total is None else total + folded
            stat_ref[pl.ds(blocks + i * here + b, 1), :] = jnp.sum(total.T, axis=0, keepdims=True)
        return 0

    lax.fori_loop(0, rows // step, block, 0)
    kernel_copy.wait()


def student_softmax(audio, text, kernel):
    rows, columns, depth = audio.shape[0], text.shape[0], audio.shape[1]
    return pl.pallas_call(
        student_kernel,
        out_shape=(
            pltpu.VMEM((2, rows, columns), jnp.float32),
            jax.ShapeDtypeStruct((2 * (rows // LANES), LANES), jnp.float32),
        ),
        in_specs=[VMEM, pl.BlockSpec(memory_space=pltpu.HBM), pl.BlockSpec(memory_space=pltpu.HBM)],
        out_specs=(VMEM, VMEM),
        scratch_shapes=[pltpu.VMEM(text.shape, text.dtype), pltpu.SemaphoreType.DMA, pltpu.SemaphoreType.DMA],
        compiler_params=params(),
        name="student_softmax",
    )(audio, streamed(text), streamed(kernel))


def residual_kernel(
    rows_ref, scale_ref, own_ref, pair_ref, audio_ref, text_ref,
    audio_out_ref, text_out_ref, weight_ref, prob_ref, residual_ref,
):
    kernel_ref, exp_ref = pair_ref.at[0], pair_ref.at[1]
    step, depth = audio_out_ref.shape
    rows, columns = pair_ref.shape[1:]
    blocks = own_ref.shape[0] // 2
    groups = WIDTH // LANES
    i = pl.program_id(0)

    @pl.when(i == 0)
    def _():
        spread_rows(1.0 / jnp.sum(rows_ref[:, :blocks, :], axis=0), weight_ref)
        tops = rows_ref[:, blocks : 2 * blocks, :]
        top = jnp.max(tops, axis=0)
        total = jnp.sum(jnp.exp(tops - top[None]) * rows_ref[:, 2 * blocks :, :], axis=0)
        spread_rows(jnp.exp(own_ref[:blocks, :] - top) / total, prob_ref)

    at = pl.ds(pl.multiple_of(i * step, step), step)
    for j in range(columns // WIDTH):
        lanes = pl.ds(j * WIDTH, WIDTH)
        scale = spread_cols(scale_ref[j * groups : (j + 1) * groups, :])
        scale = jnp.concatenate([scale] * (step // 8), axis=0)
        target = (repeat_lanes(weight_ref[at, :], groups) * kernel_ref[at, lanes]) * scale
        prob = exp_ref[at, lanes] * repeat_lanes(prob_ref[at, :], groups)
        residual_ref[at, lanes] = (prob - target).astype(jnp.bfloat16)
    audio_out_ref[...] = 10.0 * jnp.dot(residual_ref[at, :], text_ref[...], preferred_element_type=jnp.float32)

    @pl.when(i == pl.num_programs(0) - 1)
    def _():
        for j in range(columns // WIDTH):
            grad = lax.dot_general(
                residual_ref[:, pl.ds(j * WIDTH, WIDTH)],
                audio_ref[...],
                (((0,), (0,)), ((), ())),
                preferred_element_type=jnp.float32,
            )
            text_out_ref[pl.ds(j * WIDTH, WIDTH), :] = (10.0 * grad).astype(text_out_ref.dtype)


def residual_grads(row_parts, scale, own, pair, audio, text, dtype):
    rows, columns = pair.shape[1:]
    depth = audio.shape[1]
    step = 256
    return pl.pallas_call(
        residual_kernel,
        grid=(rows // step,),
        out_shape=(
            jax.ShapeDtypeStruct((rows, depth), jnp.float32),
            pltpu.VMEM((columns, depth), dtype),
        ),
        in_specs=[VMEM] * 6,
        out_specs=(pl.BlockSpec((step, depth), lambda i: (i, 0)), VMEM),
        scratch_shapes=[
            pltpu.VMEM((rows, LANES), jnp.float32),
            pltpu.VMEM((rows, LANES), jnp.float32),
            pltpu.VMEM((rows, columns), jnp.bfloat16),
        ],
        compiler_params=params(19 * 1024 * 1024),
        name="residual_grads",
    )(row_parts, scale, own, resident(pair), audio, text)


def resident(x):
    return pltpu.with_memory_space_constraint(x, pltpu.VMEM)


def streamed(x):
    return pltpu.with_memory_space_constraint(x, pltpu.HBM)


def gather_a2a(x, axis, n):
    spread = jnp.broadcast_to(x[None], (n, *x.shape))
    return lax.all_to_all(spread, axis, 0, 0).reshape(n * x.shape[0], x.shape[1])


def swap(x, axis):
    return lax.all_to_all(x, axis, 0, 0)


def body(clips, caps, teacher_audio, teacher_text, student_audio, student_text):
    count, depth = teacher_audio.shape
    audio = jnp.concatenate([teacher_audio, student_audio], axis=0)
    audio = lax.all_gather(audio, "cap", axis=0)
    text_t = gather_a2a(teacher_text, "clip", clips)
    probe = text_t[:16, :LANES]
    student_text, probe = lax.optimization_barrier((student_text, probe))
    text_s = lax.all_gather(student_text, "clip", axis=0, tiled=True)
    audio_t = audio[:, :count].reshape(-1, depth)
    audio_s = audio[:, count:].reshape(-1, depth)
    logits, maxima = teacher_logits(audio_t, text_t, probe, caps)
    kernel, columns = exp_columns(swap(maxima, "cap"), logits, clips)
    for _ in range(ITERS - 1):
        row_parts, _ = row_sums(swap(columns, "clip"), kernel, caps)
        columns = column_sums(swap(row_parts, "cap"), kernel, clips)
    columns, text_s, audio_s = lax.optimization_barrier((columns, text_s, audio_s))
    columns, audio_s = lax.optimization_barrier((swap(columns, "clip"), audio_s))
    pair, stats = student_softmax(audio_s, text_s, kernel)
    row_parts, scale = row_sums(columns, pair, caps, stats)
    row_parts = swap(row_parts, "cap")
    audio_part, text_part = residual_grads(
        row_parts, scale, stats, pair, audio_s, text_s, jnp.bfloat16
    )
    audio_grad = lax.psum_scatter(audio_part, "cap", scatter_dimension=0, tiled=True)
    text_parts = swap(text_part.reshape(clips, -1, text_part.shape[1]), "clip")
    text_grad = jnp.sum(text_parts.astype(jnp.float32), axis=0)
    return audio_grad, text_grad


def solution(mesh):
    placed = (
        P(("clip", "cap"), None),
        P(("cap", "clip"), None),
        P(("clip", "cap"), None),
        P(("cap", "clip"), None),
    )
    return jax.shard_map(
        functools.partial(body, mesh.shape["clip"], mesh.shape["cap"]),
        mesh=mesh,
        in_specs=placed,
        out_specs=(P(("clip", "cap"), None), P(("cap", "clip"), None)),
        check_vma=False,
    )
```

```python
import functools

import jax
import jax.numpy as jnp
from jax import lax
from jax.experimental import pallas as pl
from jax.experimental.pallas import tpu as pltpu
from jax.sharding import PartitionSpec as P

ITERS = 3
LANES = 128
WIDTH = 512
VMEM = pl.BlockSpec(memory_space=pltpu.VMEM)
LIMIT = 19 * 1024 * 1024


def params(limit=LIMIT):
    return pltpu.CompilerParams(vmem_limit_bytes=limit)


def lanes_of(ref, block):
    return ref[pl.ds(block * LANES, LANES), :].T


def spread_rows(vec, ref):
    for block in range(vec.shape[0]):
        row = jnp.broadcast_to(vec[block : block + 1, :], (LANES, LANES))
        ref[pl.ds(block * LANES, LANES), :] = row.T


def spread_cols(vec):
    return jnp.concatenate(
        [jnp.broadcast_to(vec[g : g + 1, :], (8, LANES)) for g in range(vec.shape[0])], axis=1
    )


def repeat_lanes(col, groups):
    return jnp.concatenate([col] * groups, axis=1)


def fold_lanes(x, op):
    parts = [x[:, g * LANES : (g + 1) * LANES] for g in range(x.shape[1] // LANES)]
    while len(parts) > 1:
        parts = [op(*parts[k : k + 2]) if k + 1 < len(parts) else parts[k] for k in range(0, len(parts), 2)]
    return parts[0]


def contract_last(left, right):
    return lax.dot_general(left, right, (((1,), (1,)), ((), ())), preferred_element_type=jnp.float32)


def logits_kernel(audio_ref, text_ref, probe_ref, logits_ref, max_ref, part_ref):
    rows, columns = logits_ref.shape
    step = 2 * audio_ref.shape[1]

    def block(i, _):
        base = pl.multiple_of(i * step, step)
        left = audio_ref[pl.ds(2 * i, 2)].reshape(step, audio_ref.shape[2])
        best = None
        for j in range(columns // WIDTH):
            at = j * WIDTH
            x = 10.0 * contract_last(left, text_ref[pl.ds(at, WIDTH), :])
            logits_ref[pl.ds(base, step), pl.ds(at, WIDTH)] = x
            folded = fold_lanes(x, jnp.maximum)
            best = folded if best is None else jnp.maximum(best, folded)
        part_ref[pl.ds(base, step), :] = best
        return 0

    lax.fori_loop(0, rows // step, block, 0)
    for b in range(rows // LANES):
        top = jnp.max(lanes_of(part_ref, b), axis=0, keepdims=True)
        for k in range(max_ref.shape[0]):
            max_ref[k, b : b + 1, :] = top


def audio_half(audio, half):
    shards, count, depth = audio.shape
    return pl.BlockSpec((shards, count // 2, depth), lambda i: (0, half, 0), pipeline_mode=pl.Buffered(1))


def teacher_logits(audio, text, probe, peers):
    rows, columns = audio.shape[0] * audio.shape[1] // 2, text.shape[0]
    return pl.pallas_call(
        logits_kernel,
        grid=(1,),
        out_shape=(
            pltpu.VMEM((rows, columns), jnp.float32),
            jax.ShapeDtypeStruct((peers, rows // LANES, LANES), jnp.float32),
        ),
        in_specs=[audio_half(audio, 0), VMEM, VMEM],
        out_specs=(VMEM, VMEM),
        scratch_shapes=[pltpu.VMEM((rows, LANES), jnp.float32)],
        compiler_params=params(),
        name="logits",
    )(streamed(audio), text, probe)


def put_columns(acc, sum_ref, out_ref):
    groups = sum_ref.shape[0]
    for g in range(groups):
        sum_ref[g : g + 1, :] = jnp.sum(acc[:, g * LANES : (g + 1) * LANES], axis=0, keepdims=True)
    total = sum_ref[...]
    for k in range(out_ref.shape[0]):
        out_ref[k] = total


def exp_kernel(max_ref, logits_ref, kernel_ref, out_ref, col_ref, sum_ref):
    rows, columns = logits_ref.shape
    spread_rows(jnp.max(max_ref[...], axis=0), col_ref)

    def step(i, acc):
        at = pl.ds(pl.multiple_of(i * 8, 8), 8)
        k = jnp.exp(logits_ref[at, :] - repeat_lanes(col_ref[at, :], columns // LANES))
        kernel_ref[at, :] = k
        return acc + k

    acc = lax.fori_loop(0, rows // 8, step, jnp.zeros((8, columns), jnp.float32), unroll=4)
    put_columns(acc, sum_ref, out_ref)


def exp_columns(maxima, logits, peers):
    rows, columns = logits.shape
    return pl.pallas_call(
        exp_kernel,
        out_shape=(
            pltpu.VMEM((rows, columns), jnp.float32),
            jax.ShapeDtypeStruct((peers, columns // LANES, LANES), jnp.float32),
        ),
        in_specs=[VMEM, VMEM],
        out_specs=(VMEM, VMEM),
        scratch_shapes=[
            pltpu.VMEM((rows, LANES), jnp.float32),
            pltpu.VMEM((columns // LANES, LANES), jnp.float32),
        ],
        input_output_aliases={1: 0},
        compiler_params=params(),
        name="exp_columns",
    )(maxima, resident(logits))


def row_kernel(parts_ref, kernel_ref, stat_ref, out_ref, scale_ref, part_ref):
    if stat_ref is not None:
        kernel_ref = kernel_ref.at[0]
    rows = kernel_ref.shape[0]
    blocks = rows // LANES
    scale_ref[...] = 1.0 / jnp.sum(parts_ref[...], axis=0)
    scale = spread_cols(scale_ref[...])

    def step(i, _):
        at = pl.ds(pl.multiple_of(i * 8, 8), 8)
        part_ref[at, :] = fold_lanes(kernel_ref[at, :] * scale, jnp.add)
        return 0

    lax.fori_loop(0, rows // 8, step, 0, unroll=4)
    for b in range(blocks):
        total = jnp.sum(lanes_of(part_ref, b), axis=0, keepdims=True)
        for k in range(out_ref.shape[0]):
            out_ref[k, b : b + 1, :] = total
    if stat_ref is not None:
        for k in range(out_ref.shape[0]):
            out_ref[k, blocks:, :] = stat_ref[...]


def row_sums(parts, kernel, peers, stats=None):
    rows, columns = kernel.shape[-2:]
    if stats is None:
        extra, body = (), lambda parts_ref, kernel_ref, *refs: row_kernel(parts_ref, kernel_ref, None, *refs)
    else:
        extra, body = (stats,), row_kernel
    return pl.pallas_call(
        body,
        out_shape=(
            jax.ShapeDtypeStruct((peers, rows // LANES * (3 if extra else 1), LANES), jnp.float32),
            jax.ShapeDtypeStruct((columns // LANES, LANES), jnp.float32),
        ),
        in_specs=[VMEM] * (2 + len(extra)),
        out_specs=(VMEM, VMEM),
        scratch_shapes=[pltpu.VMEM((rows, LANES), jnp.float32)],
        compiler_params=params(),
        name="row_sums",
    )(parts, resident(kernel), *extra)


def column_kernel(parts_ref, kernel_ref, out_ref, col_ref, sum_ref):
    rows, columns = kernel_ref.shape
    spread_rows(1.0 / jnp.sum(parts_ref[...], axis=0), col_ref)

    def step(i, acc):
        at = pl.ds(pl.multiple_of(i * 8, 8), 8)
        return acc + kernel_ref[at, :] * repeat_lanes(col_ref[at, :], columns // LANES)

    acc = lax.fori_loop(0, rows // 8, step, jnp.zeros((8, columns), jnp.float32), unroll=4)
    put_columns(acc, sum_ref, out_ref)


def column_sums(parts, kernel, peers):
    rows, columns = kernel.shape
    return pl.pallas_call(
        column_kernel,
        out_shape=jax.ShapeDtypeStruct((peers, columns // LANES, LANES), jnp.float32),
        in_specs=[VMEM, VMEM],
        out_specs=VMEM,
        scratch_shapes=[
            pltpu.VMEM((rows, LANES), jnp.float32),
            pltpu.VMEM((columns // LANES, LANES), jnp.float32),
        ],
        compiler_params=params(),
        name="column_sums",
    )(parts, resident(kernel))


def student_kernel(audio_ref, text_hbm_ref, kernel_hbm_ref, pair_ref, stat_ref, text_ref, text_sem, kernel_sem):
    kernel_ref, exp_ref = pair_ref.at[0], pair_ref.at[1]
    rows, columns = pair_ref.shape[1:]
    text_copy = pltpu.make_async_copy(text_hbm_ref, text_ref, text_sem)
    kernel_copy = pltpu.make_async_copy(kernel_hbm_ref, kernel_ref, kernel_sem)
    text_copy.start()
    text_copy.wait()
    kernel_copy.start()
    step = 2 * audio_ref.shape[1]
    here = step // LANES
    blocks = rows // LANES

    def block(i, _):
        base = pl.multiple_of(i * step, step)
        left = audio_ref[pl.ds(2 * i, 2)].reshape(step, audio_ref.shape[2])
        best = None
        for j in range(columns // WIDTH):
            x = 10.0 * contract_last(left, text_ref[pl.ds(j * WIDTH, WIDTH), :])
            exp_ref[pl.ds(base, step), pl.ds(j * WIDTH, WIDTH)] = x
            folded = fold_lanes(x, jnp.maximum)
            best = folded if best is None else jnp.maximum(best, folded)
        for b in range(here):
            at = pl.ds(pl.multiple_of(base + b * LANES, LANES), LANES)
            top = jnp.max(best[b * LANES : (b + 1) * LANES, :].T, axis=0, keepdims=True)
            stat_ref[pl.ds(i * here + b, 1), :] = top
            top = repeat_lanes(jnp.broadcast_to(top, (LANES, LANES)).T, WIDTH // LANES)
            total = None
            for j in range(columns // WIDTH):
                e = jnp.exp(exp_ref[at, pl.ds(j * WIDTH, WIDTH)] - top)
                exp_ref[at, pl.ds(j * WIDTH, WIDTH)] = e
                folded = fold_lanes(e, jnp.add)
                total = folded if total is None else total + folded
            stat_ref[pl.ds(blocks + i * here + b, 1), :] = jnp.sum(total.T, axis=0, keepdims=True)
        return 0

    lax.fori_loop(0, rows // step, block, 0)
    kernel_copy.wait()


def student_softmax(audio, text, kernel):
    rows, columns = audio.shape[0] * audio.shape[1] // 2, text.shape[0]
    return pl.pallas_call(
        student_kernel,
        grid=(1,),
        out_shape=(
            pltpu.VMEM((2, rows, columns), jnp.float32),
            jax.ShapeDtypeStruct((2 * (rows // LANES), LANES), jnp.float32),
        ),
        in_specs=[audio_half(audio, 1), pl.BlockSpec(memory_space=pltpu.HBM), pl.BlockSpec(memory_space=pltpu.HBM)],
        out_specs=(VMEM, VMEM),
        scratch_shapes=[pltpu.VMEM(text.shape, text.dtype), pltpu.SemaphoreType.DMA, pltpu.SemaphoreType.DMA],
        compiler_params=params(),
        name="student_softmax",
    )(streamed(audio), streamed(text), streamed(kernel))


def residual_kernel(
    rows_ref, scale_ref, own_ref, pair_ref, audio_ref, text_ref,
    audio_out_ref, text_out_ref, weight_ref, prob_ref, residual_ref,
):
    kernel_ref, exp_ref = pair_ref.at[0], pair_ref.at[1]
    step, depth = audio_out_ref.shape
    rows, columns = pair_ref.shape[1:]
    blocks = own_ref.shape[0] // 2
    groups = WIDTH // LANES
    i = pl.program_id(0)

    @pl.when(i == 0)
    def _():
        spread_rows(1.0 / jnp.sum(rows_ref[:, :blocks, :], axis=0), weight_ref)
        tops = rows_ref[:, blocks : 2 * blocks, :]
        top = jnp.max(tops, axis=0)
        total = jnp.sum(jnp.exp(tops - top[None]) * rows_ref[:, 2 * blocks :, :], axis=0)
        spread_rows(jnp.exp(own_ref[:blocks, :] - top) / total, prob_ref)

    at = pl.ds(pl.multiple_of(i * step, step), step)
    for j in range(columns // WIDTH):
        lanes = pl.ds(j * WIDTH, WIDTH)
        scale = spread_cols(scale_ref[j * groups : (j + 1) * groups, :])
        scale = jnp.concatenate([scale] * (step // 8), axis=0)
        target = (repeat_lanes(weight_ref[at, :], groups) * kernel_ref[at, lanes]) * scale
        prob = exp_ref[at, lanes] * repeat_lanes(prob_ref[at, :], groups)
        residual_ref[at, lanes] = (prob - target).astype(jnp.bfloat16)
    audio_out_ref[...] = 10.0 * jnp.dot(residual_ref[at, :], text_ref[...], preferred_element_type=jnp.float32)

    @pl.when(i == pl.num_programs(0) - 1)
    def _():
        audio = audio_ref[...].reshape(rows, depth)
        for j in range(columns // WIDTH):
            grad = lax.dot_general(
                residual_ref[:, pl.ds(j * WIDTH, WIDTH)],
                audio,
                (((0,), (0,)), ((), ())),
                preferred_element_type=jnp.float32,
            )
            text_out_ref[pl.ds(j * WIDTH, WIDTH), :] = (10.0 * grad).astype(text_out_ref.dtype)


def residual_grads(row_parts, scale, own, pair, audio, text, dtype):
    rows, columns = pair.shape[1:]
    depth = audio.shape[2]
    step = 256
    return pl.pallas_call(
        residual_kernel,
        grid=(rows // step,),
        out_shape=(
            jax.ShapeDtypeStruct((rows, depth), jnp.float32),
            pltpu.VMEM((columns, depth), dtype),
        ),
        in_specs=[VMEM] * 4 + [audio_half(audio, 1), VMEM],
        out_specs=(pl.BlockSpec((step, depth), lambda i: (i, 0)), VMEM),
        scratch_shapes=[
            pltpu.VMEM((rows, LANES), jnp.float32),
            pltpu.VMEM((rows, LANES), jnp.float32),
            pltpu.VMEM((rows, columns), jnp.bfloat16),
        ],
        compiler_params=params(19 * 1024 * 1024),
        name="residual_grads",
    )(row_parts, scale, own, resident(pair), streamed(audio), text)


def resident(x):
    return pltpu.with_memory_space_constraint(x, pltpu.VMEM)


def streamed(x):
    return pltpu.with_memory_space_constraint(x, pltpu.HBM)


def gather_a2a(x, axis, n):
    spread = jnp.broadcast_to(x[None], (n, *x.shape))
    return lax.all_to_all(spread, axis, 0, 0).reshape(n * x.shape[0], x.shape[1])


def swap(x, axis):
    return lax.all_to_all(x, axis, 0, 0)


def body(clips, caps, teacher_audio, teacher_text, student_audio, student_text):
    audio = jnp.concatenate([teacher_audio, student_audio], axis=0)
    audio = lax.all_gather(audio, "cap", axis=0)
    text_t = gather_a2a(teacher_text, "clip", clips)
    probe = text_t[:16, :LANES]
    student_text, probe = lax.optimization_barrier((student_text, probe))
    text_s = lax.all_gather(student_text, "clip", axis=0, tiled=True)
    logits, maxima = teacher_logits(audio, text_t, probe, caps)
    kernel, columns = exp_columns(swap(maxima, "cap"), logits, clips)
    for _ in range(ITERS - 1):
        row_parts, _ = row_sums(swap(columns, "clip"), kernel, caps)
        columns = column_sums(swap(row_parts, "cap"), kernel, clips)
    columns, text_s = lax.optimization_barrier((columns, text_s))
    columns, audio = lax.optimization_barrier((swap(columns, "clip"), audio))
    pair, stats = student_softmax(audio, text_s, kernel)
    row_parts, scale = row_sums(columns, pair, caps, stats)
    row_parts = swap(row_parts, "cap")
    audio_part, text_part = residual_grads(
        row_parts, scale, stats, pair, audio, text_s, jnp.bfloat16
    )
    audio_grad = lax.psum_scatter(audio_part, "cap", scatter_dimension=0, tiled=True)
    text_parts = swap(text_part.reshape(clips, -1, text_part.shape[1]), "clip")
    text_grad = jnp.sum(text_parts.astype(jnp.float32), axis=0)
    return audio_grad, text_grad


def solution(mesh):
    placed = (
        P(("clip", "cap"), None),
        P(("cap", "clip"), None),
        P(("clip", "cap"), None),
        P(("cap", "clip"), None),
    )
    return jax.shard_map(
        functools.partial(body, mesh.shape["clip"], mesh.shape["cap"]),
        mesh=mesh,
        in_specs=placed,
        out_specs=(P(("clip", "cap"), None), P(("cap", "clip"), None)),
        check_vma=False,
    )
```

```python
import functools

import jax
import jax.numpy as jnp
from jax import lax
from jax.experimental import pallas as pl
from jax.experimental.pallas import tpu as pltpu
from jax.sharding import PartitionSpec as P

ITERS = 3
LANES = 128
WIDTH = 512
VMEM = pl.BlockSpec(memory_space=pltpu.VMEM)
LIMIT = 19 * 1024 * 1024


def params(limit=LIMIT):
    return pltpu.CompilerParams(vmem_limit_bytes=limit)


def lanes_of(ref, block):
    return ref[pl.ds(block * LANES, LANES), :].T


def spread_rows(vec, ref):
    for block in range(vec.shape[0]):
        row = jnp.broadcast_to(vec[block : block + 1, :], (LANES, LANES))
        ref[pl.ds(block * LANES, LANES), :] = row.T


def spread_cols(vec):
    return jnp.concatenate(
        [jnp.broadcast_to(vec[g : g + 1, :], (8, LANES)) for g in range(vec.shape[0])], axis=1
    )


def repeat_lanes(col, groups):
    return jnp.concatenate([col] * groups, axis=1)


def fold_lanes(x, op):
    parts = [x[:, g * LANES : (g + 1) * LANES] for g in range(x.shape[1] // LANES)]
    while len(parts) > 1:
        parts = [op(*parts[k : k + 2]) if k + 1 < len(parts) else parts[k] for k in range(0, len(parts), 2)]
    return parts[0]


def contract_last(left, right):
    return lax.dot_general(left, right, (((1,), (1,)), ((), ())), preferred_element_type=jnp.float32)


def logits_kernel(audio_ref, text_ref, probe_ref, logits_ref, max_ref, part_ref):
    rows, columns = logits_ref.shape
    step = 2 * audio_ref.shape[1]

    def block(i, _):
        base = pl.multiple_of(i * step, step)
        left = audio_ref[pl.ds(2 * i, 2)].reshape(step, audio_ref.shape[2])
        best = None
        for j in range(columns // WIDTH):
            at = j * WIDTH
            x = 10.0 * contract_last(left, text_ref[pl.ds(at, WIDTH), :])
            logits_ref[pl.ds(base, step), pl.ds(at, WIDTH)] = x
            folded = fold_lanes(x, jnp.maximum)
            best = folded if best is None else jnp.maximum(best, folded)
        part_ref[pl.ds(base, step), :] = best
        return 0

    lax.fori_loop(0, rows // step, block, 0)
    for b in range(rows // LANES):
        top = jnp.max(lanes_of(part_ref, b), axis=0, keepdims=True)
        for k in range(max_ref.shape[0]):
            max_ref[k, b : b + 1, :] = top


def audio_half(audio, half):
    shards, count, depth = audio.shape
    return pl.BlockSpec((shards, count // 2, depth), lambda i: (0, half, 0), pipeline_mode=pl.Buffered(1))


def teacher_logits(audio, text, probe, peers):
    rows, columns = audio.shape[0] * audio.shape[1] // 2, text.shape[0]
    return pl.pallas_call(
        logits_kernel,
        grid=(1,),
        out_shape=(
            pltpu.VMEM((rows, columns), jnp.float32),
            jax.ShapeDtypeStruct((peers, rows // LANES, LANES), jnp.float32),
        ),
        in_specs=[audio_half(audio, 0), VMEM, VMEM],
        out_specs=(VMEM, VMEM),
        scratch_shapes=[pltpu.VMEM((rows, LANES), jnp.float32)],
        compiler_params=params(),
        name="logits",
    )(streamed(audio), text, probe)


def put_columns(acc, sum_ref, out_ref):
    groups = sum_ref.shape[0]
    for g in range(groups):
        sum_ref[g : g + 1, :] = jnp.sum(acc[:, g * LANES : (g + 1) * LANES], axis=0, keepdims=True)
    total = sum_ref[...]
    for k in range(out_ref.shape[0]):
        out_ref[k] = total


def exp_kernel(max_ref, logits_ref, kernel_ref, out_ref, col_ref, sum_ref):
    rows, columns = logits_ref.shape
    spread_rows(jnp.max(max_ref[...], axis=0), col_ref)

    def step(i, acc):
        at = pl.ds(pl.multiple_of(i * 8, 8), 8)
        k = jnp.exp(logits_ref[at, :] - repeat_lanes(col_ref[at, :], columns // LANES))
        kernel_ref[at, :] = k
        return acc + k

    acc = lax.fori_loop(0, rows // 8, step, jnp.zeros((8, columns), jnp.float32), unroll=4)
    put_columns(acc, sum_ref, out_ref)


def exp_columns(maxima, logits, peers):
    rows, columns = logits.shape
    return pl.pallas_call(
        exp_kernel,
        out_shape=(
            pltpu.VMEM((rows, columns), jnp.float32),
            jax.ShapeDtypeStruct((peers, columns // LANES, LANES), jnp.float32),
        ),
        in_specs=[VMEM, VMEM],
        out_specs=(VMEM, VMEM),
        scratch_shapes=[
            pltpu.VMEM((rows, LANES), jnp.float32),
            pltpu.VMEM((columns // LANES, LANES), jnp.float32),
        ],
        input_output_aliases={1: 0},
        compiler_params=params(),
        name="exp_columns",
    )(maxima, resident(logits))


def row_kernel(parts_ref, kernel_ref, stat_ref, out_ref, scale_ref, part_ref):
    if stat_ref is not None:
        kernel_ref = kernel_ref.at[0]
    rows = kernel_ref.shape[0]
    blocks = rows // LANES
    scale_ref[...] = 1.0 / jnp.sum(parts_ref[...], axis=0)
    scale = spread_cols(scale_ref[...])

    def step(i, _):
        at = pl.ds(pl.multiple_of(i * 8, 8), 8)
        part_ref[at, :] = fold_lanes(kernel_ref[at, :] * scale, jnp.add)
        return 0

    lax.fori_loop(0, rows // 8, step, 0, unroll=4)
    for b in range(blocks):
        total = jnp.sum(lanes_of(part_ref, b), axis=0, keepdims=True)
        for k in range(out_ref.shape[0]):
            out_ref[k, b : b + 1, :] = total
    if stat_ref is not None:
        for k in range(out_ref.shape[0]):
            out_ref[k, blocks:, :] = stat_ref[...]


def row_sums(parts, kernel, peers, stats=None):
    rows, columns = kernel.shape[-2:]
    if stats is None:
        extra, body = (), lambda parts_ref, kernel_ref, *refs: row_kernel(parts_ref, kernel_ref, None, *refs)
    else:
        extra, body = (stats,), row_kernel
    return pl.pallas_call(
        body,
        out_shape=(
            jax.ShapeDtypeStruct((peers, rows // LANES * (3 if extra else 1), LANES), jnp.float32),
            jax.ShapeDtypeStruct((columns // LANES, LANES), jnp.float32),
        ),
        in_specs=[VMEM] * (2 + len(extra)),
        out_specs=(VMEM, VMEM),
        scratch_shapes=[pltpu.VMEM((rows, LANES), jnp.float32)],
        compiler_params=params(),
        name="row_sums",
    )(parts, resident(kernel), *extra)


def column_kernel(parts_ref, kernel_ref, out_ref, col_ref, sum_ref):
    rows, columns = kernel_ref.shape
    spread_rows(1.0 / jnp.sum(parts_ref[...], axis=0), col_ref)

    def step(i, acc):
        at = pl.ds(pl.multiple_of(i * 8, 8), 8)
        return acc + kernel_ref[at, :] * repeat_lanes(col_ref[at, :], columns // LANES)

    acc = lax.fori_loop(0, rows // 8, step, jnp.zeros((8, columns), jnp.float32), unroll=4)
    put_columns(acc, sum_ref, out_ref)


def column_sums(parts, kernel, peers):
    rows, columns = kernel.shape
    return pl.pallas_call(
        column_kernel,
        out_shape=jax.ShapeDtypeStruct((peers, columns // LANES, LANES), jnp.float32),
        in_specs=[VMEM, VMEM],
        out_specs=VMEM,
        scratch_shapes=[
            pltpu.VMEM((rows, LANES), jnp.float32),
            pltpu.VMEM((columns // LANES, LANES), jnp.float32),
        ],
        compiler_params=params(),
        name="column_sums",
    )(parts, resident(kernel))


def student_kernel(audio_ref, text_hbm_ref, kernel_hbm_ref, pair_ref, stat_ref, text_ref, text_sem, kernel_sem):
    kernel_ref, exp_ref = pair_ref.at[0], pair_ref.at[1]
    rows, columns = pair_ref.shape[1:]
    text_copy = pltpu.make_async_copy(text_hbm_ref, text_ref, text_sem)
    kernel_copy = pltpu.make_async_copy(kernel_hbm_ref, kernel_ref, kernel_sem)
    text_copy.start()
    text_copy.wait()
    kernel_copy.start()
    step = 2 * audio_ref.shape[1]
    here = step // LANES
    blocks = rows // LANES

    def block(i, _):
        base = pl.multiple_of(i * step, step)
        left = audio_ref[pl.ds(2 * i, 2)].reshape(step, audio_ref.shape[2])
        best = None
        for j in range(columns // WIDTH):
            x = 10.0 * contract_last(left, text_ref[pl.ds(j * WIDTH, WIDTH), :])
            exp_ref[pl.ds(base, step), pl.ds(j * WIDTH, WIDTH)] = x
            folded = fold_lanes(x, jnp.maximum)
            best = folded if best is None else jnp.maximum(best, folded)
        for b in range(here):
            at = pl.ds(pl.multiple_of(base + b * LANES, LANES), LANES)
            top = jnp.max(best[b * LANES : (b + 1) * LANES, :].T, axis=0, keepdims=True)
            stat_ref[pl.ds(i * here + b, 1), :] = top
            top = repeat_lanes(jnp.broadcast_to(top, (LANES, LANES)).T, WIDTH // LANES)
            total = None
            for j in range(columns // WIDTH):
                e = jnp.exp(exp_ref[at, pl.ds(j * WIDTH, WIDTH)] - top)
                exp_ref[at, pl.ds(j * WIDTH, WIDTH)] = e
                folded = fold_lanes(e, jnp.add)
                total = folded if total is None else total + folded
            stat_ref[pl.ds(blocks + i * here + b, 1), :] = jnp.sum(total.T, axis=0, keepdims=True)
        return 0

    lax.fori_loop(0, rows // step, block, 0)
    kernel_copy.wait()


def student_softmax(audio, text, kernel):
    rows, columns = audio.shape[0] * audio.shape[1] // 2, text.shape[0]
    return pl.pallas_call(
        student_kernel,
        grid=(1,),
        out_shape=(
            pltpu.VMEM((2, rows, columns), jnp.float32),
            jax.ShapeDtypeStruct((2 * (rows // LANES), LANES), jnp.float32),
        ),
        in_specs=[audio_half(audio, 1), pl.BlockSpec(memory_space=pltpu.HBM), pl.BlockSpec(memory_space=pltpu.HBM)],
        out_specs=(VMEM, VMEM),
        scratch_shapes=[pltpu.VMEM(text.shape, text.dtype), pltpu.SemaphoreType.DMA, pltpu.SemaphoreType.DMA],
        compiler_params=params(),
        name="student_softmax",
    )(streamed(audio), streamed(text), streamed(kernel))


def residual_kernel(
    rows_ref, scale_ref, own_ref, pair_ref, audio_ref, text_ref,
    audio_out_ref, text_out_ref, weight_ref, prob_ref, residual_ref,
):
    kernel_ref, exp_ref = pair_ref.at[0], pair_ref.at[1]
    step, depth = audio_out_ref.shape
    rows, columns = pair_ref.shape[1:]
    blocks = own_ref.shape[0] // 2
    groups = WIDTH // LANES
    i = pl.program_id(0)

    @pl.when(i == 0)
    def _():
        spread_rows(1.0 / jnp.sum(rows_ref[:, :blocks, :], axis=0), weight_ref)
        tops = rows_ref[:, blocks : 2 * blocks, :]
        top = jnp.max(tops, axis=0)
        total = jnp.sum(jnp.exp(tops - top[None]) * rows_ref[:, 2 * blocks :, :], axis=0)
        spread_rows(jnp.exp(own_ref[:blocks, :] - top) / total, prob_ref)

    at = pl.ds(pl.multiple_of(i * step, step), step)
    for j in range(columns // WIDTH):
        lanes = pl.ds(j * WIDTH, WIDTH)
        scale = spread_cols(scale_ref[j * groups : (j + 1) * groups, :])
        scale = jnp.concatenate([scale] * (step // 8), axis=0)
        target = (repeat_lanes(weight_ref[at, :], groups) * kernel_ref[at, lanes]) * scale
        prob = exp_ref[at, lanes] * repeat_lanes(prob_ref[at, :], groups)
        residual_ref[at, lanes] = (prob - target).astype(jnp.bfloat16)
    audio_out_ref[...] = 10.0 * jnp.dot(residual_ref[at, :], text_ref[...], preferred_element_type=jnp.float32)

    @pl.when(i == pl.num_programs(0) - 1)
    def _():
        audio = audio_ref[...].reshape(rows, depth)
        for j in range(columns // WIDTH):
            grad = lax.dot_general(
                residual_ref[:, pl.ds(j * WIDTH, WIDTH)],
                audio,
                (((0,), (0,)), ((), ())),
                preferred_element_type=jnp.float32,
            )
            text_out_ref[pl.ds(j * WIDTH, WIDTH), :] = (10.0 * grad).astype(text_out_ref.dtype)


def residual_grads(row_parts, scale, own, pair, audio, text, dtype):
    rows, columns = pair.shape[1:]
    depth = audio.shape[2]
    step = audio.shape[1]
    return pl.pallas_call(
        residual_kernel,
        grid=(rows // step,),
        out_shape=(
            jax.ShapeDtypeStruct((rows, depth), jnp.float32),
            pltpu.VMEM((columns, depth), dtype),
        ),
        in_specs=[VMEM] * 4 + [audio_half(audio, 1), VMEM],
        out_specs=(pl.BlockSpec((step, depth), lambda i: (i, 0)), VMEM),
        scratch_shapes=[
            pltpu.VMEM((rows, LANES), jnp.float32),
            pltpu.VMEM((rows, LANES), jnp.float32),
            pltpu.VMEM((rows, columns), jnp.bfloat16),
        ],
        compiler_params=params(19 * 1024 * 1024),
        name="residual_grads",
    )(row_parts, scale, own, resident(pair), streamed(audio), text)


def resident(x):
    return pltpu.with_memory_space_constraint(x, pltpu.VMEM)


def streamed(x):
    return pltpu.with_memory_space_constraint(x, pltpu.HBM)


def gather_a2a(x, axis, n):
    spread = jnp.broadcast_to(x[None], (n, *x.shape))
    return lax.all_to_all(spread, axis, 0, 0).reshape(n * x.shape[0], x.shape[1])


def swap(x, axis):
    return lax.all_to_all(x, axis, 0, 0)


def body(clips, caps, teacher_audio, teacher_text, student_audio, student_text):
    audio = jnp.concatenate([teacher_audio, student_audio], axis=0)
    audio = lax.all_gather(audio, "cap", axis=0)
    text_t = gather_a2a(teacher_text, "clip", clips)
    probe = text_t[:16, :LANES]
    student_text, probe = lax.optimization_barrier((student_text, probe))
    text_s = lax.all_gather(student_text, "clip", axis=0, tiled=True)
    logits, maxima = teacher_logits(audio, text_t, probe, caps)
    kernel, columns = exp_columns(swap(maxima, "cap"), logits, clips)
    for _ in range(ITERS - 1):
        row_parts, _ = row_sums(swap(columns, "clip"), kernel, caps)
        columns = column_sums(swap(row_parts, "cap"), kernel, clips)
    columns, text_s = lax.optimization_barrier((columns, text_s))
    columns, audio = lax.optimization_barrier((swap(columns, "clip"), audio))
    pair, stats = student_softmax(audio, text_s, kernel)
    row_parts, scale = row_sums(columns, pair, caps, stats)
    row_parts = swap(row_parts, "cap")
    audio_part, text_part = residual_grads(
        row_parts, scale, stats, pair, audio, text_s, jnp.bfloat16
    )
    audio_grad = lax.psum_scatter(audio_part, "cap", scatter_dimension=0, tiled=True)
    text_parts = swap(text_part.reshape(clips, -1, text_part.shape[1]), "clip")
    text_grad = jnp.sum(text_parts.astype(jnp.float32), axis=0)
    return audio_grad, text_grad


def solution(mesh):
    placed = (
        P(("clip", "cap"), None),
        P(("cap", "clip"), None),
        P(("clip", "cap"), None),
        P(("cap", "clip"), None),
    )
    return jax.shard_map(
        functools.partial(body, mesh.shape["clip"], mesh.shape["cap"]),
        mesh=mesh,
        in_specs=placed,
        out_specs=(P(("clip", "cap"), None), P(("cap", "clip"), None)),
        check_vma=False,
    )
```

```python
import functools

import jax
import jax.numpy as jnp
from jax import lax
from jax.experimental import pallas as pl
from jax.experimental.pallas import tpu as pltpu
from jax.sharding import PartitionSpec as P

ITERS = 3
LANES = 128
WIDTH = 512
VMEM = pl.BlockSpec(memory_space=pltpu.VMEM)
LIMIT = 19 * 1024 * 1024


def params(limit=LIMIT):
    return pltpu.CompilerParams(vmem_limit_bytes=limit)


def lanes_of(ref, block):
    return ref[pl.ds(block * LANES, LANES), :].T


def spread_rows(vec, ref):
    for block in range(vec.shape[0]):
        row = jnp.broadcast_to(vec[block : block + 1, :], (LANES, LANES))
        ref[pl.ds(block * LANES, LANES), :] = row.T


def spread_cols(vec):
    return jnp.concatenate(
        [jnp.broadcast_to(vec[g : g + 1, :], (8, LANES)) for g in range(vec.shape[0])], axis=1
    )


def repeat_lanes(col, groups):
    return jnp.concatenate([col] * groups, axis=1)


def fold_lanes(x, op):
    parts = [x[:, g * LANES : (g + 1) * LANES] for g in range(x.shape[1] // LANES)]
    while len(parts) > 1:
        parts = [op(*parts[k : k + 2]) if k + 1 < len(parts) else parts[k] for k in range(0, len(parts), 2)]
    return parts[0]


def contract_last(left, right):
    return lax.dot_general(left, right, (((1,), (1,)), ((), ())), preferred_element_type=jnp.float32)


def logits_kernel(audio_ref, text_ref, probe_ref, logits_ref, max_ref, part_ref):
    rows, columns = logits_ref.shape
    step = 2 * audio_ref.shape[1]

    def block(i, _):
        base = pl.multiple_of(i * step, step)
        left = audio_ref[pl.ds(2 * i, 2)].reshape(step, audio_ref.shape[2])
        best = None
        for j in range(columns // WIDTH):
            at = j * WIDTH
            x = 10.0 * contract_last(left, text_ref[pl.ds(at, WIDTH), :])
            logits_ref[pl.ds(base, step), pl.ds(at, WIDTH)] = x
            folded = fold_lanes(x, jnp.maximum)
            best = folded if best is None else jnp.maximum(best, folded)
        part_ref[pl.ds(base, step), :] = best
        return 0

    lax.fori_loop(0, rows // step, block, 0)
    for b in range(rows // LANES):
        top = jnp.max(lanes_of(part_ref, b), axis=0, keepdims=True)
        for k in range(max_ref.shape[0]):
            max_ref[k, b : b + 1, :] = top


def audio_half(audio, half):
    shards, count, depth = audio.shape
    return pl.BlockSpec((shards, count // 2, depth), lambda i: (0, half, 0), pipeline_mode=pl.Buffered(1))


def teacher_logits(audio, text, probe, peers):
    rows, columns = audio.shape[0] * audio.shape[1] // 2, text.shape[0]
    return pl.pallas_call(
        logits_kernel,
        grid=(1,),
        out_shape=(
            pltpu.VMEM((rows, columns), jnp.float32),
            jax.ShapeDtypeStruct((peers, rows // LANES, LANES), jnp.float32),
        ),
        in_specs=[audio_half(audio, 0), VMEM, VMEM],
        out_specs=(VMEM, VMEM),
        scratch_shapes=[pltpu.VMEM((rows, LANES), jnp.float32)],
        compiler_params=params(),
        name="logits",
    )(streamed(audio), text, probe)


def put_columns(acc, sum_ref, out_ref):
    groups = sum_ref.shape[0]
    for g in range(groups):
        sum_ref[g : g + 1, :] = jnp.sum(acc[:, g * LANES : (g + 1) * LANES], axis=0, keepdims=True)
    total = sum_ref[...]
    for k in range(out_ref.shape[0]):
        out_ref[k] = total


def exp_kernel(max_ref, logits_ref, kernel_ref, out_ref, col_ref, sum_ref):
    rows, columns = logits_ref.shape
    spread_rows(jnp.max(max_ref[...], axis=0), col_ref)

    def step(i, acc):
        at = pl.ds(pl.multiple_of(i * 8, 8), 8)
        k = jnp.exp(logits_ref[at, :] - repeat_lanes(col_ref[at, :], columns // LANES))
        kernel_ref[at, :] = k
        return acc + k

    acc = lax.fori_loop(0, rows // 8, step, jnp.zeros((8, columns), jnp.float32), unroll=8)
    put_columns(acc, sum_ref, out_ref)


def exp_columns(maxima, logits, peers):
    rows, columns = logits.shape
    return pl.pallas_call(
        exp_kernel,
        out_shape=(
            pltpu.VMEM((rows, columns), jnp.float32),
            jax.ShapeDtypeStruct((peers, columns // LANES, LANES), jnp.float32),
        ),
        in_specs=[VMEM, VMEM],
        out_specs=(VMEM, VMEM),
        scratch_shapes=[
            pltpu.VMEM((rows, LANES), jnp.float32),
            pltpu.VMEM((columns // LANES, LANES), jnp.float32),
        ],
        input_output_aliases={1: 0},
        compiler_params=params(),
        name="exp_columns",
    )(maxima, resident(logits))


def row_kernel(parts_ref, kernel_ref, stat_ref, out_ref, scale_ref, part_ref):
    if stat_ref is not None:
        kernel_ref = kernel_ref.at[0]
    rows = kernel_ref.shape[0]
    blocks = rows // LANES
    scale_ref[...] = 1.0 / jnp.sum(parts_ref[...], axis=0)
    scale = spread_cols(scale_ref[...])

    def step(i, _):
        at = pl.ds(pl.multiple_of(i * 8, 8), 8)
        part_ref[at, :] = fold_lanes(kernel_ref[at, :] * scale, jnp.add)
        return 0

    lax.fori_loop(0, rows // 8, step, 0, unroll=8)
    for b in range(blocks):
        total = jnp.sum(lanes_of(part_ref, b), axis=0, keepdims=True)
        for k in range(out_ref.shape[0]):
            out_ref[k, b : b + 1, :] = total
    if stat_ref is not None:
        for k in range(out_ref.shape[0]):
            out_ref[k, blocks:, :] = stat_ref[...]


def row_sums(parts, kernel, peers, stats=None):
    rows, columns = kernel.shape[-2:]
    if stats is None:
        extra, body = (), lambda parts_ref, kernel_ref, *refs: row_kernel(parts_ref, kernel_ref, None, *refs)
    else:
        extra, body = (stats,), row_kernel
    return pl.pallas_call(
        body,
        out_shape=(
            jax.ShapeDtypeStruct((peers, rows // LANES * (3 if extra else 1), LANES), jnp.float32),
            jax.ShapeDtypeStruct((columns // LANES, LANES), jnp.float32),
        ),
        in_specs=[VMEM] * (2 + len(extra)),
        out_specs=(VMEM, VMEM),
        scratch_shapes=[pltpu.VMEM((rows, LANES), jnp.float32)],
        compiler_params=params(),
        name="row_sums",
    )(parts, resident(kernel), *extra)


def column_kernel(parts_ref, kernel_ref, out_ref, col_ref, sum_ref):
    rows, columns = kernel_ref.shape
    spread_rows(1.0 / jnp.sum(parts_ref[...], axis=0), col_ref)

    def step(i, acc):
        at = pl.ds(pl.multiple_of(i * 8, 8), 8)
        return acc + kernel_ref[at, :] * repeat_lanes(col_ref[at, :], columns // LANES)

    acc = lax.fori_loop(0, rows // 8, step, jnp.zeros((8, columns), jnp.float32), unroll=8)
    put_columns(acc, sum_ref, out_ref)


def column_sums(parts, kernel, peers):
    rows, columns = kernel.shape
    return pl.pallas_call(
        column_kernel,
        out_shape=jax.ShapeDtypeStruct((peers, columns // LANES, LANES), jnp.float32),
        in_specs=[VMEM, VMEM],
        out_specs=VMEM,
        scratch_shapes=[
            pltpu.VMEM((rows, LANES), jnp.float32),
            pltpu.VMEM((columns // LANES, LANES), jnp.float32),
        ],
        compiler_params=params(),
        name="column_sums",
    )(parts, resident(kernel))


def student_kernel(audio_ref, text_hbm_ref, kernel_hbm_ref, pair_ref, stat_ref, text_ref, text_sem, kernel_sem):
    kernel_ref, exp_ref = pair_ref.at[0], pair_ref.at[1]
    rows, columns = pair_ref.shape[1:]
    text_copy = pltpu.make_async_copy(text_hbm_ref, text_ref, text_sem)
    kernel_copy = pltpu.make_async_copy(kernel_hbm_ref, kernel_ref, kernel_sem)
    text_copy.start()
    text_copy.wait()
    kernel_copy.start()
    step = 2 * audio_ref.shape[1]
    here = step // LANES
    blocks = rows // LANES

    def block(i, _):
        base = pl.multiple_of(i * step, step)
        left = audio_ref[pl.ds(2 * i, 2)].reshape(step, audio_ref.shape[2])
        best = None
        for j in range(columns // WIDTH):
            x = 10.0 * contract_last(left, text_ref[pl.ds(j * WIDTH, WIDTH), :])
            exp_ref[pl.ds(base, step), pl.ds(j * WIDTH, WIDTH)] = x
            folded = fold_lanes(x, jnp.maximum)
            best = folded if best is None else jnp.maximum(best, folded)
        for b in range(here):
            at = pl.ds(pl.multiple_of(base + b * LANES, LANES), LANES)
            top = jnp.max(best[b * LANES : (b + 1) * LANES, :].T, axis=0, keepdims=True)
            stat_ref[pl.ds(i * here + b, 1), :] = top
            top = repeat_lanes(jnp.broadcast_to(top, (LANES, LANES)).T, WIDTH // LANES)
            total = None
            for j in range(columns // WIDTH):
                e = jnp.exp(exp_ref[at, pl.ds(j * WIDTH, WIDTH)] - top)
                exp_ref[at, pl.ds(j * WIDTH, WIDTH)] = e
                folded = fold_lanes(e, jnp.add)
                total = folded if total is None else total + folded
            stat_ref[pl.ds(blocks + i * here + b, 1), :] = jnp.sum(total.T, axis=0, keepdims=True)
        return 0

    lax.fori_loop(0, rows // step, block, 0)
    kernel_copy.wait()


def student_softmax(audio, text, kernel):
    rows, columns = audio.shape[0] * audio.shape[1] // 2, text.shape[0]
    return pl.pallas_call(
        student_kernel,
        grid=(1,),
        out_shape=(
            pltpu.VMEM((2, rows, columns), jnp.float32),
            jax.ShapeDtypeStruct((2 * (rows // LANES), LANES), jnp.float32),
        ),
        in_specs=[audio_half(audio, 1), pl.BlockSpec(memory_space=pltpu.HBM), pl.BlockSpec(memory_space=pltpu.HBM)],
        out_specs=(VMEM, VMEM),
        scratch_shapes=[pltpu.VMEM(text.shape, text.dtype), pltpu.SemaphoreType.DMA, pltpu.SemaphoreType.DMA],
        compiler_params=params(),
        name="student_softmax",
    )(streamed(audio), streamed(text), streamed(kernel))


def residual_kernel(
    rows_ref, scale_ref, own_ref, pair_ref, audio_ref, text_ref,
    audio_out_ref, text_out_ref, weight_ref, prob_ref, residual_ref,
):
    kernel_ref, exp_ref = pair_ref.at[0], pair_ref.at[1]
    step, depth = audio_out_ref.shape
    rows, columns = pair_ref.shape[1:]
    blocks = own_ref.shape[0] // 2
    groups = WIDTH // LANES
    i = pl.program_id(0)

    @pl.when(i == 0)
    def _():
        spread_rows(1.0 / jnp.sum(rows_ref[:, :blocks, :], axis=0), weight_ref)
        tops = rows_ref[:, blocks : 2 * blocks, :]
        top = jnp.max(tops, axis=0)
        total = jnp.sum(jnp.exp(tops - top[None]) * rows_ref[:, 2 * blocks :, :], axis=0)
        spread_rows(jnp.exp(own_ref[:blocks, :] - top) / total, prob_ref)

    at = pl.ds(pl.multiple_of(i * step, step), step)
    for j in range(columns // WIDTH):
        lanes = pl.ds(j * WIDTH, WIDTH)
        scale = spread_cols(scale_ref[j * groups : (j + 1) * groups, :])
        scale = jnp.concatenate([scale] * (step // 8), axis=0)
        target = (repeat_lanes(weight_ref[at, :], groups) * kernel_ref[at, lanes]) * scale
        prob = exp_ref[at, lanes] * repeat_lanes(prob_ref[at, :], groups)
        residual_ref[at, lanes] = (prob - target).astype(jnp.bfloat16)
    audio_out_ref[...] = 10.0 * jnp.dot(residual_ref[at, :], text_ref[...], preferred_element_type=jnp.float32)

    @pl.when(i == pl.num_programs(0) - 1)
    def _():
        audio = audio_ref[...].reshape(rows, depth)
        for j in range(columns // WIDTH):
            grad = lax.dot_general(
                residual_ref[:, pl.ds(j * WIDTH, WIDTH)],
                audio,
                (((0,), (0,)), ((), ())),
                preferred_element_type=jnp.float32,
            )
            text_out_ref[pl.ds(j * WIDTH, WIDTH), :] = (10.0 * grad).astype(text_out_ref.dtype)


def residual_grads(row_parts, scale, own, pair, audio, text, dtype):
    rows, columns = pair.shape[1:]
    depth = audio.shape[2]
    step = 256
    return pl.pallas_call(
        residual_kernel,
        grid=(rows // step,),
        out_shape=(
            jax.ShapeDtypeStruct((rows, depth), jnp.float32),
            pltpu.VMEM((columns, depth), dtype),
        ),
        in_specs=[VMEM] * 4 + [audio_half(audio, 1), VMEM],
        out_specs=(pl.BlockSpec((step, depth), lambda i: (i, 0)), VMEM),
        scratch_shapes=[
            pltpu.VMEM((rows, LANES), jnp.float32),
            pltpu.VMEM((rows, LANES), jnp.float32),
            pltpu.VMEM((rows, columns), jnp.bfloat16),
        ],
        compiler_params=params(19 * 1024 * 1024),
        name="residual_grads",
    )(row_parts, scale, own, resident(pair), streamed(audio), text)


def resident(x):
    return pltpu.with_memory_space_constraint(x, pltpu.VMEM)


def streamed(x):
    return pltpu.with_memory_space_constraint(x, pltpu.HBM)


def gather_a2a(x, axis, n):
    spread = jnp.broadcast_to(x[None], (n, *x.shape))
    return lax.all_to_all(spread, axis, 0, 0).reshape(n * x.shape[0], x.shape[1])


def swap(x, axis):
    return lax.all_to_all(x, axis, 0, 0)


def body(clips, caps, teacher_audio, teacher_text, student_audio, student_text):
    audio = jnp.concatenate([teacher_audio, student_audio], axis=0)
    audio = lax.all_gather(audio, "cap", axis=0)
    text_t = gather_a2a(teacher_text, "clip", clips)
    probe = text_t[:16, :LANES]
    student_text, probe = lax.optimization_barrier((student_text, probe))
    text_s = lax.all_gather(student_text, "clip", axis=0, tiled=True)
    logits, maxima = teacher_logits(audio, text_t, probe, caps)
    kernel, columns = exp_columns(swap(maxima, "cap"), logits, clips)
    for _ in range(ITERS - 1):
        row_parts, _ = row_sums(swap(columns, "clip"), kernel, caps)
        columns = column_sums(swap(row_parts, "cap"), kernel, clips)
    columns, text_s = lax.optimization_barrier((columns, text_s))
    columns, audio = lax.optimization_barrier((swap(columns, "clip"), audio))
    pair, stats = student_softmax(audio, text_s, kernel)
    row_parts, scale = row_sums(columns, pair, caps, stats)
    row_parts = swap(row_parts, "cap")
    audio_part, text_part = residual_grads(
        row_parts, scale, stats, pair, audio, text_s, jnp.bfloat16
    )
    audio_grad = lax.psum_scatter(audio_part, "cap", scatter_dimension=0, tiled=True)
    text_parts = swap(text_part.reshape(clips, -1, text_part.shape[1]), "clip")
    text_grad = jnp.sum(text_parts.astype(jnp.float32), axis=0)
    return audio_grad, text_grad


def solution(mesh):
    placed = (
        P(("clip", "cap"), None),
        P(("cap", "clip"), None),
        P(("clip", "cap"), None),
        P(("cap", "clip"), None),
    )
    return jax.shard_map(
        functools.partial(body, mesh.shape["clip"], mesh.shape["cap"]),
        mesh=mesh,
        in_specs=placed,
        out_specs=(P(("clip", "cap"), None), P(("cap", "clip"), None)),
        check_vma=False,
    )
```
